32 devices in a mesh: groups: 2 (over x), blk: 8 (over z, y), head: 2 (over core).
Axes of the slice: x: 2, y: 2, z: 4, core: 2. Of those that a mesh axis runs over, the one named last changes fastest.
Arguments:
- queries: bfloat16 [1024, 36864], P(('groups', 'blk'), 'head'), parts along dimension 0, may hold values from -750 to 750
- latent_cache: bfloat16 [128, 576, 256], P(('groups', 'blk')), parts along dimension 0, may hold values from -6 to 6
- new_latent: bfloat16 [576, 1024], P(None, ('groups', 'blk')), parts along dimension 1, may hold values from -6 to 6
- span_len: int32 [16], P('groups'), parts along dimension 0, may hold values from 2 to 57, as said below
- dec_count: int32 [16], P('groups'), parts along dimension 0, may hold values from 1 to 7, as said below
- span_start: int32 [16], P(('groups', 'blk')), parts along dimension 0, may hold values from 0 to 256, as said below
- cache_len: int32 [16, 7], P(('groups', 'blk')), parts along dimension 0, may hold values from 2 to 256, as said below
- value_weight: bfloat16 [64, 512, 128], P('head'), may hold values from -0.25 to 0.25
- out_weight: bfloat16 [8192, 7168], P('head', 'blk'), may hold values from -0.0625 to 0.0625
- residual: bfloat16 [1024, 7168], P(('groups', 'blk')), parts along dimension 0, may hold values from -34 to 34
- norm_gain: float32 [7168], replicated, may hold values from 0.1 to 1.9
- gate_weight: bfloat16 [7168, 9216], P(None, ('blk', 'head')), may hold values from -0.0625 to 0.0625
- up_weight: bfloat16 [7168, 9216], P(None, ('blk', 'head')), may hold values from -0.0625 to 0.0625
- down_weight: bfloat16 [9216, 7168], P(('blk', 'head')), may hold values from -0.0625 to 0.0625
Outputs:
- mixed: bfloat16 [1024, 7168], P(('groups', 'blk', 'head')), parts along dimension 0
The draws below stay inside these ranges and needn't reach their ends.
There are 2 independent parts, one for each index of `groups`. The reference program is written for one: setup_inputs(seed, part) draws one part's arguments, and reference() takes and returns one part's arrays. A program takes and returns all parts, laid end to end along the dimension named above; an argument that names none is the same for every part. Nothing has to cross between parts.
Inputs may be any that keep to these rules, and one draw needn't show every extreme that they name: span_len + dec_count is at most 64 on every rank, exactly 64 on one rank, at most 32 on every other rank and exactly 32 on some other rank; its sum over all ranks is exactly 256. `dec_count`: decode row j of a rank uses the rank's sequence slot j + 1. `span_start`: the cached positions of a rank's sequence slot 0. `cache_len`: entry j belongs to sequence slot j + 1; entries at or past a rank's dec_count are unused.
All inputs are finite; a program needn't handle non-finite values.
Results may differ from the reference program's by a relative error of at most 0.02.
Values may be sent and summed in bfloat16 or wider, within the bound.
A program may use at most 128 MiB of HBM per device.

```python
import jax
import jax.numpy as jnp
from jax import lax

D = 7168
FF = 9216
HEADS = 64
KV = 512
VH = 128
ROWS_DEV = 64
SEQ_DEV = 8
CACHE = 256
LAT = 576
RANKS = 8
ROWS = 512
SEQS = 64
SHARDS = 16


def serving_plan(key):
    base_key = jax.random.fold_in(key, 7001)
    keys_all = jax.random.split(base_key, 5)
    ranking = jax.random.permutation(keys_all[0], RANKS)
    busiest = ranking[0]
    lightest = ranking[1]
    fullest = ranking[2]
    half_rows = ROWS_DEV // 2
    rank_ids = jnp.arange(RANKS, dtype=jnp.int32)
    weights_int = jax.random.randint(keys_all[1], (RANKS,), 1, 8)
    weights_int = jnp.where((rank_ids == busiest) | (rank_ids == fullest), 0, weights_int)
    losses = weights_int * half_rows // jnp.sum(weights_int)
    shortfall = half_rows - jnp.sum(losses)
    places = jnp.argsort(ranking)
    losses = losses + ((places >= 3) & (places <= shortfall + 2)).astype(jnp.int32)
    lives = jnp.where(rank_ids == busiest, ROWS_DEV, half_rows - losses)
    decode = jax.random.randint(keys_all[2], (RANKS,), 1, SEQ_DEV)
    decode = jnp.minimum(decode, lives - 2)
    decode = jnp.where(rank_ids == busiest, SEQ_DEV - 1, decode)
    decode = jnp.where(rank_ids == lightest, 1, decode)
    spans = lives - decode
    starts = jax.random.randint(keys_all[3], (RANKS,), 0, CACHE + 1)
    starts = jnp.where(rank_ids == lightest, 0, starts)
    starts = jnp.where(rank_ids == busiest, CACHE, starts)
    lengths = jax.random.randint(keys_all[4], (RANKS, SEQ_DEV - 1), 2, CACHE + 1)
    lengths = lengths.at[busiest, 0].set(CACHE)
    lengths = lengths.at[lightest, 0].set(2)
    return (spans.astype(jnp.int32), decode.astype(jnp.int32), starts.astype(jnp.int32), lengths.astype(jnp.int32))


def float_inputs(key):
    float_key = jax.random.fold_in(key, 9001)
    keys_all = jax.random.split(float_key, 3)
    latent_cache = jnp.clip(jax.random.normal(keys_all[0], (SEQS, LAT, CACHE), jnp.float32), -6.0, 6.0)
    new_latent = jnp.clip(jax.random.normal(keys_all[1], (LAT, ROWS), jnp.float32), -6.0, 6.0)
    queries = jnp.clip(jax.random.normal(keys_all[2], (ROWS, HEADS, LAT), jnp.float32), -6.0, 6.0)
    return (queries.reshape(ROWS, HEADS * LAT), latent_cache, new_latent)


def draw_queries(key, part):
    return float_inputs(key)[0].astype(jnp.bfloat16)


def draw_latent_cache(key, part):
    return float_inputs(key)[1].astype(jnp.bfloat16)


def draw_new_latent(key, part):
    return float_inputs(key)[2].astype(jnp.bfloat16)


def draw_span_len(key, part):
    return serving_plan(key)[0]


def draw_dec_count(key, part):
    return serving_plan(key)[1]


def draw_span_start(key, part):
    return serving_plan(key)[2]


def draw_cache_len(key, part):
    return serving_plan(key)[3]


def draw_residual(key, part):
    keys_all = jax.random.split(jax.random.fold_in(key, 4242), 1)
    values = jnp.clip(jax.random.normal(keys_all[0], (ROWS, D), jnp.float32), -6.0, 6.0) * 0.5
    return values.astype(jnp.bfloat16)


def steps_of(stream_key, dims, cuts, low, largest):
    gain, own = 1.0, jax.random.fold_in(stream_key, 6)
    for dim, blocks in cuts:
        steps = jnp.exp(jax.random.uniform(jax.random.fold_in(own, dim), (blocks,), jnp.float32, low / len(cuts), largest / len(cuts)))
        gain = gain * jnp.repeat(steps, dims[dim] // blocks).reshape([-1 if axis == dim else 1 for axis in range(len(dims))])
    return gain


def scatter_about(key, dims, deviation, limit, cuts=(), held_as=jnp.bfloat16):
    array = jax.random.normal(key, dims, jnp.float32) * deviation
    if len(cuts) > 0:
        array = steps_of(key, dims, cuts, -0.22, 0.18) * array
    return jnp.clip(array, min=-limit, max=limit).astype(held_as)


def setup_inputs(seed: int = 0, part: int = 0) -> dict:
    streams_of = jax.random.split(jax.random.key(seed), 15)
    part_keys = jax.random.split(jax.random.fold_in(streams_of[14], part), 15)
    queries = draw_queries(jax.random.fold_in(jax.random.fold_in(streams_of[14], part), 71), part)
    latent_cache = draw_latent_cache(jax.random.fold_in(jax.random.fold_in(streams_of[14], part), 71), part)
    new_latent = draw_new_latent(jax.random.fold_in(jax.random.fold_in(streams_of[14], part), 71), part)
    span_len = draw_span_len(jax.random.fold_in(jax.random.fold_in(streams_of[14], part), 71), part)
    dec_count = draw_dec_count(jax.random.fold_in(jax.random.fold_in(streams_of[14], part), 71), part)
    span_start = draw_span_start(jax.random.fold_in(jax.random.fold_in(streams_of[14], part), 71), part)
    cache_len = draw_cache_len(jax.random.fold_in(jax.random.fold_in(streams_of[14], part), 71), part)
    value_weight = scatter_about(streams_of[7], (HEADS, KV, VH), KV ** -0.5, 0.25, ((0, 2),))
    out_weight = scatter_about(streams_of[8], (HEADS * VH, D), (HEADS * VH) ** -0.5, 0.0625, ((0, 2), (1, 8)))
    residual = draw_residual(jax.random.fold_in(jax.random.fold_in(streams_of[14], part), 71), part)
    norm_gain = jnp.clip(1.0 + 0.18 * jax.random.normal(streams_of[10], (D,), jnp.float32), 0.1, 1.9)
    gate_weight = scatter_about(streams_of[11], (D, FF), D ** -0.5, 0.0625, ((1, 16),))
    up_weight = scatter_about(streams_of[12], (D, FF), D ** -0.5, 0.0625, ((1, 16),))
    down_weight = scatter_about(streams_of[13], (FF, D), FF ** -0.5, 0.0625, ((0, 16),))
    return dict(queries=queries, latent_cache=latent_cache, new_latent=new_latent, span_len=span_len, dec_count=dec_count, span_start=span_start, cache_len=cache_len, value_weight=value_weight, out_weight=out_weight, residual=residual, norm_gain=norm_gain, gate_weight=gate_weight, up_weight=up_weight, down_weight=down_weight)


score_scale = 192.0 ** (-0.5)
norm_eps = 1e-06
masked_score = -1e+30

def rounded(values):
    return lax.optimization_barrier(values.astype(jnp.bfloat16)).astype(jnp.float32)

def rank_attention(rank_index, queries, latent_cache, new_latent, span_len, dec_count, span_start, cache_len, value_weight):
    row_slots = lax.dynamic_slice_in_dim(queries, (rank_index * ROWS_DEV).astype(jnp.int32), ROWS_DEV, 0)
    query_rows = row_slots.reshape(ROWS_DEV, HEADS, LAT).astype(jnp.float32)
    cache_slots = lax.dynamic_slice_in_dim(latent_cache, (rank_index * SEQ_DEV).astype(jnp.int32), SEQ_DEV, 0).astype(jnp.float32)
    fresh_keys = lax.dynamic_slice_in_dim(new_latent, (rank_index * ROWS_DEV).astype(jnp.int32), ROWS_DEV, 1).astype(jnp.float32)
    span_rows = span_len[rank_index]
    decode_rows = dec_count[rank_index]
    start_pos = span_start[rank_index]
    lengths = cache_len[rank_index]
    positions = jnp.arange(CACHE, dtype=jnp.int32)
    local_rows = jnp.arange(ROWS_DEV, dtype=jnp.int32)
    cached_scores = jnp.einsum('rhl,lt->rht', query_rows, cache_slots[0]) * score_scale
    fresh_scores = jnp.einsum('rhl,lj->rhj', query_rows, fresh_keys) * score_scale
    cached_seen = (positions < start_pos)[None, None, :]
    fresh_seen = (local_rows[None, :] <= local_rows[:, None])[:, None, :]
    cached_scores = jnp.where(cached_seen, cached_scores, masked_score)
    fresh_scores = jnp.where(fresh_seen, fresh_scores, masked_score)
    peak_score = jnp.maximum(lax.optimization_barrier(jnp.max(cached_scores, axis=2)), lax.optimization_barrier(jnp.max(fresh_scores, axis=2)))[:, :, None]
    cached_exp = jnp.where(cached_seen, jnp.exp(cached_scores - peak_score), 0.0)
    fresh_exp = jnp.where(fresh_seen, jnp.exp(fresh_scores - peak_score), 0.0)
    totals = lax.optimization_barrier(jnp.sum(cached_exp, axis=2, keepdims=True)) + lax.optimization_barrier(jnp.sum(fresh_exp, axis=2, keepdims=True))
    span_out = jnp.einsum('rht,lt->rhl', rounded(cached_exp / totals), cache_slots[0, :KV])
    span_out = span_out + jnp.einsum('rhj,lj->rhl', rounded(fresh_exp / totals), fresh_keys[:KV])
    decode_slots = jnp.arange(SEQ_DEV - 1, dtype=jnp.int32)
    decode_index = jnp.clip(span_rows + decode_slots, 0, ROWS_DEV - 1).astype(jnp.int32)
    decode_query = query_rows[decode_index]
    decode_keys = cache_slots[1:]
    own_keys = fresh_keys[:, decode_index]
    slot_scores = jnp.einsum('shl,slt->sht', decode_query, decode_keys) * score_scale
    slot_seen = (positions[None, :] < lengths[:, None])[:, None, :]
    slot_scores = jnp.where(slot_seen, slot_scores, masked_score)
    own_scores = jnp.einsum('shl,ls->sh', decode_query, own_keys) * score_scale
    slot_peak = jnp.maximum(lax.optimization_barrier(jnp.max(slot_scores, axis=2)), own_scores)
    slot_exp = jnp.where(slot_seen, jnp.exp(slot_scores - slot_peak[:, :, None]), 0.0)
    own_exp = jnp.exp(own_scores - slot_peak)
    slot_totals = lax.optimization_barrier(jnp.sum(slot_exp, axis=2)) + own_exp
    decode_out = jnp.einsum('sht,slt->shl', rounded(slot_exp / slot_totals[:, :, None]), decode_keys[:, :KV])
    decode_out = decode_out + rounded(own_exp / slot_totals)[:, :, None] * own_keys[:KV].T[:, None, :]
    placing = ((local_rows[:, None] == span_rows + decode_slots[None, :]) & (decode_slots[None, :] < decode_rows)).astype(jnp.float32)
    latent_out = jnp.where((local_rows < span_rows)[:, None, None], span_out, 0.0)
    latent_out = latent_out + jnp.einsum('is,shl->ihl', placing, decode_out)
    head_values = jnp.einsum('rhl,hlv->rhv', rounded(latent_out), value_weight.astype(jnp.float32))
    return head_values.astype(jnp.bfloat16).reshape(ROWS_DEV, HEADS * VH)

def reference(queries, latent_cache, new_latent, span_len, dec_count, span_start, cache_len, value_weight, out_weight, residual, norm_gain, gate_weight, up_weight, down_weight):
    rank_ids = jnp.arange(RANKS, dtype=jnp.int32)
    head_values = lax.map(lambda rank_index: rank_attention(rank_index, queries, latent_cache, new_latent, span_len, dec_count, span_start, cache_len, value_weight), rank_ids)
    head_values = head_values.reshape(ROWS, HEADS * VH)
    attended = jnp.dot(head_values, out_weight, preferred_element_type=jnp.float32)
    stream = residual.astype(jnp.float32) + attended
    scale_rows = lax.rsqrt(lax.optimization_barrier(jnp.mean(stream * stream, axis=1, keepdims=True)) + norm_eps)
    normed = (stream * scale_rows * norm_gain[None, :]).astype(jnp.bfloat16)
    gate_values = jnp.dot(normed, gate_weight, preferred_element_type=jnp.float32)
    up_values = jnp.dot(normed, up_weight, preferred_element_type=jnp.float32)
    hidden = (jax.nn.silu(gate_values) * up_values).astype(jnp.bfloat16)
    block_width = FF // SHARDS

    def add_block(block_index, running):
        begin = (block_index * block_width).astype(jnp.int32)
        part_hidden = lax.dynamic_slice_in_dim(hidden, begin, block_width, 1)
        part_down = lax.dynamic_slice_in_dim(down_weight, begin, block_width, 0)
        return running + rounded(jnp.dot(part_hidden, part_down, preferred_element_type=jnp.float32))
    projected = lax.fori_loop(0, SHARDS, add_block, jnp.zeros((ROWS, D), jnp.float32))
    lives = span_len + dec_count
    slot_ids = jnp.arange(ROWS, dtype=jnp.int32)
    owners = slot_ids // ROWS_DEV
    live_rows = slot_ids % ROWS_DEV < lives[owners]
    return jnp.where(live_rows[:, None], stream + projected, 0.0).astype(jnp.bfloat16)
```

```python
import jax
import jax.numpy as jnp
from jax import lax
from jax.sharding import PartitionSpec as P

score_scale = 192.0 ** (-0.5)
norm_eps = 1e-06
masked_score = -1e30


def rounded(values):
    return lax.optimization_barrier(values.astype(jnp.bfloat16)).astype(jnp.float32)


def pick_rank(values, rank_index):
    matches = jnp.arange(values.shape[0], dtype=jnp.int32) == rank_index
    return jnp.sum(jnp.where(matches, values, 0))


def local_attention(
    query_rows, cache_slots, fresh_keys, span_rows, decode_rows, start_pos, lengths, key_width
):
    row_count = query_rows.shape[0]
    slot_count = cache_slots.shape[0]
    positions = jnp.arange(cache_slots.shape[2], dtype=jnp.int32)
    local_rows = jnp.arange(row_count, dtype=jnp.int32)
    cached_scores = (
        jnp.einsum("rhl,lt->rht", query_rows, cache_slots[0], preferred_element_type=jnp.float32)
        * score_scale
    )
    fresh_scores = (
        jnp.einsum("rhl,lj->rhj", query_rows, fresh_keys, preferred_element_type=jnp.float32)
        * score_scale
    )
    cached_seen = (positions < start_pos)[None, None, :]
    fresh_seen = (local_rows[None, :] <= local_rows[:, None])[:, None, :]
    cached_scores = jnp.where(cached_seen, cached_scores, masked_score)
    fresh_scores = jnp.where(fresh_seen, fresh_scores, masked_score)
    peak_score = jnp.maximum(jnp.max(cached_scores, axis=2), jnp.max(fresh_scores, axis=2))[
        :, :, None
    ]
    cached_exp = jnp.where(cached_seen, jnp.exp(cached_scores - peak_score), 0.0)
    fresh_exp = jnp.where(fresh_seen, jnp.exp(fresh_scores - peak_score), 0.0)
    totals = jnp.sum(cached_exp, axis=2, keepdims=True) + jnp.sum(fresh_exp, axis=2, keepdims=True)
    span_out = jnp.einsum(
        "rht,lt->rhl",
        (cached_exp / totals).astype(jnp.bfloat16),
        cache_slots[0, :key_width],
        preferred_element_type=jnp.float32,
    )
    span_out = span_out + jnp.einsum(
        "rhj,lj->rhl",
        (fresh_exp / totals).astype(jnp.bfloat16),
        fresh_keys[:key_width],
        preferred_element_type=jnp.float32,
    )
    decode_slots = jnp.arange(slot_count - 1, dtype=jnp.int32)
    decode_index = jnp.clip(span_rows + decode_slots, 0, row_count - 1)
    decode_query = jnp.take(query_rows, decode_index, axis=0)
    decode_keys = cache_slots[1:]
    own_keys = jnp.take(fresh_keys, decode_index, axis=1)
    slot_scores = (
        jnp.einsum("shl,slt->sht", decode_query, decode_keys, preferred_element_type=jnp.float32)
        * score_scale
    )
    slot_seen = (positions[None, :] < lengths[:, None])[:, None, :]
    slot_scores = jnp.where(slot_seen, slot_scores, masked_score)
    own_scores = (
        jnp.einsum("shl,ls->sh", decode_query, own_keys, preferred_element_type=jnp.float32)
        * score_scale
    )
    slot_peak = jnp.maximum(jnp.max(slot_scores, axis=2), own_scores)
    slot_exp = jnp.where(slot_seen, jnp.exp(slot_scores - slot_peak[:, :, None]), 0.0)
    own_exp = jnp.exp(own_scores - slot_peak)
    slot_totals = jnp.sum(slot_exp, axis=2) + own_exp
    decode_out = jnp.einsum(
        "sht,slt->shl",
        (slot_exp / slot_totals[:, :, None]).astype(jnp.bfloat16),
        decode_keys[:, :key_width],
        preferred_element_type=jnp.float32,
    )
    decode_out = (
        decode_out
        + rounded(own_exp / slot_totals)[:, :, None]
        * own_keys[:key_width].T.astype(jnp.float32)[:, None, :]
    )
    placing = (
        (local_rows[:, None] == span_rows + decode_slots[None, :])
        & (decode_slots[None, :] < decode_rows)
    ).astype(jnp.float32)
    latent_out = jnp.where((local_rows < span_rows)[:, None, None], span_out, 0.0)
    latent_out = latent_out + jnp.einsum("is,shl->ihl", placing, decode_out)
    return latent_out.astype(jnp.bfloat16)


def on_device(
    queries,
    latent_cache,
    new_latent,
    span_len,
    dec_count,
    span_start,
    cache_len,
    value_weight,
    out_weight,
    residual,
    norm_gain,
    gate_weight,
    up_weight,
    down_weight,
):
    rank_index = lax.axis_index("blk")
    rows_dev = residual.shape[0]
    heads_here = value_weight.shape[0]
    lives = span_len + dec_count
    query_rows = queries.reshape(rows_dev, heads_here, queries.shape[1] // heads_here)
    latent_out = local_attention(
        query_rows,
        latent_cache,
        new_latent,
        pick_rank(span_len, rank_index),
        pick_rank(dec_count, rank_index),
        span_start[0],
        cache_len[0],
        value_weight.shape[1],
    )
    head_values = jnp.einsum(
        "rhl,hlv->rhv", latent_out, value_weight, preferred_element_type=jnp.float32
    )
    head_values = head_values.astype(jnp.bfloat16).reshape(
        rows_dev, heads_here * value_weight.shape[2]
    )
    first = rows_dev // 2
    is_full = pick_rank(lives, rank_index) > first
    width = out_weight.shape[1]
    ranks = lax.axis_size("blk")
    moved = lax.all_to_all(
        residual.reshape(rows_dev, ranks, width).transpose(1, 0, 2),
        "blk",
        split_axis=0,
        concat_axis=0,
        tiled=True,
    )
    full_ranks = (lives > first)[:, None, None]
    residual_rows = jnp.concatenate(
        [
            moved[:, :first].reshape(ranks * first, width).astype(jnp.float32),
            jnp.sum(jnp.where(full_ranks, moved[:, first:], 0).astype(jnp.float32), axis=0),
        ]
    )
    rest = jnp.where(is_full, head_values[first:], 0).astype(jnp.bfloat16)
    packed = jnp.concatenate(
        [
            lax.all_gather(head_values[:first], "blk", axis=0, tiled=True),
            lax.psum(rest, "blk"),
        ]
    )
    partial_out = jnp.dot(packed, out_weight, preferred_element_type=jnp.float32)
    attended = lax.psum(partial_out.astype(jnp.bfloat16), "head").astype(jnp.float32)
    stream = lax.all_gather(
        (residual_rows + attended).astype(jnp.bfloat16), "blk", axis=1, tiled=True
    )
    wide = stream.astype(jnp.float32)
    scale_rows = lax.rsqrt(jnp.mean(wide * wide, axis=1, keepdims=True) + norm_eps)
    normed = (wide * scale_rows * norm_gain[None, :]).astype(jnp.bfloat16)
    gate_values = jnp.dot(normed, gate_weight, preferred_element_type=jnp.float32)
    up_values = jnp.dot(normed, up_weight, preferred_element_type=jnp.float32)
    hidden = (jax.nn.silu(gate_values) * up_values).astype(jnp.bfloat16)
    partial = jnp.dot(hidden, down_weight, preferred_element_type=jnp.float32).astype(jnp.bfloat16)
    head_index = lax.axis_index("head")
    owned = lax.all_gather(
        lax.psum_scatter(partial[: ranks * first], ("blk", "head"), scatter_dimension=0, tiled=True),
        "head",
        axis=0,
        tiled=True,
    )
    spare = lax.psum(partial[ranks * first :], ("blk", "head"))
    projected = jnp.where(head_index == 0, owned, spare).astype(jnp.float32)
    place = jnp.where(head_index == 0, rank_index, ranks) * first
    stream_half = lax.dynamic_slice_in_dim(stream, place, first, 0).astype(jnp.float32)
    own_rows = head_index * first + jnp.arange(first, dtype=jnp.int32)
    alive = own_rows < pick_rank(lives, rank_index)
    return jnp.where(alive[:, None], stream_half + projected, 0.0).astype(jnp.bfloat16)


def solution(mesh):
    placed = (
        P(("groups", "blk"), "head"),
        P(("groups", "blk"), None, None),
        P(None, ("groups", "blk")),
        P("groups"),
        P("groups"),
        P(("groups", "blk")),
        P(("groups", "blk"), None),
        P("head", None, None),
        P("head", "blk"),
        P(("groups", "blk"), None),
        P(),
        P(None, ("blk", "head")),
        P(None, ("blk", "head")),
        P(("blk", "head"), None),
    )
    return jax.shard_map(
        on_device,
        mesh=mesh,
        in_specs=placed,
        out_specs=P(("groups", "blk", "head"), None),
        check_vma=False,
    )
```

```python
import jax
import jax.numpy as jnp
from jax import lax
from jax.experimental import pallas as pl
from jax.experimental.pallas import tpu as pltpu
from jax.sharding import PartitionSpec as P
import functools

score_scale = 192.0 ** (-0.5)
norm_eps = 1e-06
masked_score = -1e30


def rounded(values):
    return lax.optimization_barrier(values.astype(jnp.bfloat16)).astype(jnp.float32)


def pick_rank(values, rank_index):
    matches = jnp.arange(values.shape[0], dtype=jnp.int32) == rank_index
    return jnp.sum(jnp.where(matches, values, 0))


def local_attention(
    query_rows, cache_slots, fresh_keys, span_rows, decode_rows, start_pos, lengths, key_width
):
    row_count = query_rows.shape[0]
    slot_count = cache_slots.shape[0]
    positions = jnp.arange(cache_slots.shape[2], dtype=jnp.int32)
    local_rows = jnp.arange(row_count, dtype=jnp.int32)
    cached_scores = (
        jnp.einsum("rhl,lt->rht", query_rows, cache_slots[0], preferred_element_type=jnp.float32)
        * score_scale
    )
    fresh_scores = (
        jnp.einsum("rhl,lj->rhj", query_rows, fresh_keys, preferred_element_type=jnp.float32)
        * score_scale
    )
    cached_seen = (positions < start_pos)[None, None, :]
    fresh_seen = (local_rows[None, :] <= local_rows[:, None])[:, None, :]
    cached_scores = jnp.where(cached_seen, cached_scores, masked_score)
    fresh_scores = jnp.where(fresh_seen, fresh_scores, masked_score)
    peak_score = jnp.maximum(jnp.max(cached_scores, axis=2), jnp.max(fresh_scores, axis=2))[
        :, :, None
    ]
    cached_exp = jnp.where(cached_seen, jnp.exp(cached_scores - peak_score), 0.0)
    fresh_exp = jnp.where(fresh_seen, jnp.exp(fresh_scores - peak_score), 0.0)
    totals = jnp.sum(cached_exp, axis=2, keepdims=True) + jnp.sum(fresh_exp, axis=2, keepdims=True)
    span_out = jnp.einsum(
        "rht,lt->rhl",
        (cached_exp / totals).astype(jnp.bfloat16),
        cache_slots[0, :key_width],
        preferred_element_type=jnp.float32,
    )
    span_out = span_out + jnp.einsum(
        "rhj,lj->rhl",
        (fresh_exp / totals).astype(jnp.bfloat16),
        fresh_keys[:key_width],
        preferred_element_type=jnp.float32,
    )
    decode_slots = jnp.arange(slot_count - 1, dtype=jnp.int32)
    decode_index = jnp.clip(span_rows + decode_slots, 0, row_count - 1)
    decode_query = jnp.take(query_rows, decode_index, axis=0)
    decode_keys = cache_slots[1:]
    own_keys = jnp.take(fresh_keys, decode_index, axis=1)
    slot_scores = (
        jnp.einsum("shl,slt->sht", decode_query, decode_keys, preferred_element_type=jnp.float32)
        * score_scale
    )
    slot_seen = (positions[None, :] < lengths[:, None])[:, None, :]
    slot_scores = jnp.where(slot_seen, slot_scores, masked_score)
    own_scores = (
        jnp.einsum("shl,ls->sh", decode_query, own_keys, preferred_element_type=jnp.float32)
        * score_scale
    )
    slot_peak = jnp.maximum(jnp.max(slot_scores, axis=2), own_scores)
    slot_exp = jnp.where(slot_seen, jnp.exp(slot_scores - slot_peak[:, :, None]), 0.0)
    own_exp = jnp.exp(own_scores - slot_peak)
    slot_totals = jnp.sum(slot_exp, axis=2) + own_exp
    decode_out = jnp.einsum(
        "sht,slt->shl",
        (slot_exp / slot_totals[:, :, None]).astype(jnp.bfloat16),
        decode_keys[:, :key_width],
        preferred_element_type=jnp.float32,
    )
    decode_out = (
        decode_out
        + rounded(own_exp / slot_totals)[:, :, None]
        * own_keys[:key_width].T.astype(jnp.float32)[:, None, :]
    )
    placing = (
        (local_rows[:, None] == span_rows + decode_slots[None, :])
        & (decode_slots[None, :] < decode_rows)
    ).astype(jnp.float32)
    latent_out = jnp.where((local_rows < span_rows)[:, None, None], span_out, 0.0)
    latent_out = latent_out + jnp.einsum("is,shl->ihl", placing, decode_out)
    return latent_out.astype(jnp.bfloat16)


def send(src, dst, sent, landed, **device):
    return pltpu.make_async_remote_copy(
        src_ref=src,
        dst_ref=dst,
        send_sem=sent,
        recv_sem=landed,
        device_id=device,
        device_id_type=pl.DeviceIdType.MESH,
    )


class Line:
    def __init__(self, ranks):
        self.rank = lax.axis_index("blk")
        self.head = lax.axis_index("head")
        self.count = ranks // 2
        self.z = lax.div(self.rank, 2)
        self.y = lax.rem(self.rank, 2)
        self.has_up = self.z < self.count - 1
        self.has_down = self.z > 0
        self.up = self.rank + 2
        self.down = self.rank - 2
        self.across = self.rank + 1 - 2 * self.y
        self.twin = 1 - self.head

    def greet(self, with_twin):
        barrier = pltpu.get_barrier_semaphore()

        def signal(**device):
            pl.semaphore_signal(
                barrier, inc=1, device_id=device, device_id_type=pl.DeviceIdType.MESH
            )

        signal(blk=self.across)
        if with_twin:
            signal(head=self.twin)
        pl.when(self.has_up)(lambda: signal(blk=self.up))
        pl.when(self.has_down)(lambda: signal(blk=self.down))
        ends = (self.z == 0).astype(jnp.int32) + (self.z == self.count - 1).astype(jnp.int32)
        pl.semaphore_wait(barrier, (4 if with_twin else 3) - ends)


def gather_ranks(line, own, place, up_sem, down_sem, across_sem, landed, arrived, between):
    def to_up(s, src):
        slot = 2 * s + line.y
        return send(src, place(slot), up_sem.at[s], landed.at[slot], blk=line.up)

    def to_down(s, src):
        slot = 2 * s + line.y
        return send(src, place(slot), down_sem.at[s], landed.at[slot], blk=line.down)

    def to_across(s, src):
        slot = 2 * s + line.y
        return send(src, place(slot), across_sem.at[s], landed.at[slot], blk=line.across)

    pl.when(line.has_up)(lambda: to_up(line.z, own).start())
    pl.when(line.has_down)(lambda: to_down(line.z, own).start())
    to_across(line.z, own).start()
    for step in range(1, line.count):
        low, high = line.z - step, line.z + step

        @pl.when(low >= 0)
        def _():
            held = place(2 * low + line.y)
            to_up(low, held).wait_recv()
            pl.when(line.has_up)(lambda: to_up(low, held).start())
            to_across(low, held).start()
            arrived(2 * low + line.y)

        @pl.when(high < line.count)
        def _():
            held = place(2 * high + line.y)
            to_down(high, held).wait_recv()
            pl.when(line.has_down)(lambda: to_down(high, held).start())
            to_across(high, held).start()
            arrived(2 * high + line.y)

        between(step)
    for s in range(line.count):
        slot = 2 * s + 1 - line.y
        send(place(slot), place(slot), across_sem.at[s], landed.at[slot], blk=line.across).wait_recv()
        arrived(slot)
    for s in range(line.count):
        held = place(2 * s + line.y)
        to_across(s, held).wait_send()
        pl.when(line.has_up & (s <= line.z))(lambda: to_up(s, held).wait_send())
        pl.when(line.has_down & (s >= line.z))(lambda: to_down(s, held).wait_send())


class LineSum:
    def __init__(self, line, own, work, sent, landed):
        self.line, self.own, self.work, self.sent, self.landed = line, own, work, sent, landed

    def copy(self, src, kind, **device):
        return send(
            self.work.at[src], self.work.at[kind], self.sent.at[kind], self.landed.at[kind], **device
        )

    def step(self, index):
        line = self.line

        @pl.when(line.z == index)
        def _():
            self.work[3] = self.own()
            if index > 0:
                self.copy(3, 0, blk=line.up).wait_recv()
                self.work[3] = self.work[3] + self.work[0]
            pl.when(line.has_up)(lambda: self.copy(3, 0, blk=line.up).start())

        @pl.when(line.z == line.count - 1 - index)
        def _():
            self.work[4] = self.own()
            if index > 0:
                self.copy(4, 1, blk=line.down).wait_recv()
                self.work[4] = self.work[4] + self.work[1]
            pl.when(line.has_down)(lambda: self.copy(4, 1, blk=line.down).start())

    def column(self):
        self.work[5] = (
            self.work[3].astype(jnp.float32)
            + self.work[4].astype(jnp.float32)
            - self.own().astype(jnp.float32)
        ).astype(self.work.dtype)

    def across(self):
        return self.copy(5, 2, blk=self.line.across)

    def total(self):
        self.across().wait_recv()
        return self.work[5].astype(jnp.float32) + self.work[2].astype(jnp.float32)

    def drain(self):
        line = self.line
        self.across().wait_send()
        pl.when(line.has_up)(lambda: self.copy(3, 0, blk=line.up).wait_send())
        pl.when(line.has_down)(lambda: self.copy(4, 1, blk=line.down).wait_send())


def rows_kernel(ranks, own, rest, out, work, up_sem, down_sem, across_sem, landed, sum_sent, sum_landed):
    line = Line(ranks)
    line.greet(False)
    sums = LineSum(line, lambda: rest[...], work, sum_sent, sum_landed)
    sums.step(0)
    out[:, line.rank] = own[...]

    def between(step):
        sums.step(step)
        if step == line.count - 1:
            sums.column()
            sums.across().start()

    gather_ranks(
        line, own, lambda slot: out.at[:, slot], up_sem, down_sem, across_sem, landed,
        lambda slot: None, between,
    )
    out[:, ranks] = sums.total().astype(out.dtype)
    sums.drain()


def gather_rows(own, rest, ranks):
    halves, rows, width = own.shape
    count = ranks // 2
    dma = pltpu.SemaphoreType.DMA
    return pl.pallas_call(
        functools.partial(rows_kernel, ranks),
        out_shape=jax.ShapeDtypeStruct((halves, ranks + 1, rows, width), own.dtype),
        in_specs=[pl.BlockSpec(memory_space=pltpu.VMEM)] * 2,
        out_specs=pl.BlockSpec(memory_space=pltpu.VMEM),
        scratch_shapes=[
            pltpu.VMEM((6, halves, rows, width), own.dtype),
            dma((count,)), dma((count,)), dma((count,)), dma((ranks,)), dma((3,)), dma((3,)),
        ],
        compiler_params=pltpu.CompilerParams(
            collective_id=0, has_side_effects=True, vmem_limit_bytes=40 * 2**20
        ),
        name="gather_rows",
    )(own, rest)


def stream_kernel(
    ranks, partial, residual, out, other, mine, up_sem, down_sem, across_sem, landed, pair_sem, twin_sent, twin_landed
):
    line = Line(ranks)
    line.greet(True)
    rows, width = mine.shape
    pair = send(partial.at[line.twin], other, pair_sem.at[0], pair_sem.at[1], head=line.twin)
    pair.start()
    pair.wait_recv()
    mine[...] = (
        residual[line.head].astype(jnp.float32)
        + partial[line.head].astype(jnp.float32)
        + other[...].astype(jnp.float32)
    ).astype(mine.dtype)

    def spot(head, slot):
        if len(out.shape) == 4:
            return head, slot
        return (
            pl.ds(pl.multiple_of(head * rows, rows), rows),
            pl.ds(pl.multiple_of(slot * width, width), width),
        )

    def place(head, slot):
        return out.at[spot(head, slot)]

    def to_twin(slot, src):
        return send(
            src, place(line.head, slot), twin_sent.at[slot], twin_landed.at[slot], head=line.twin
        )

    def arrived(slot):
        to_twin(slot, place(line.head, slot)).start()

    to_twin(line.rank, mine).start()
    out[spot(line.head, line.rank)] = mine[...]
    gather_ranks(
        line, mine, lambda slot: place(line.head, slot), up_sem, down_sem, across_sem, landed,
        arrived, lambda step: None,
    )
    for slot in range(ranks):
        send(
            mine, place(line.twin, slot), twin_sent.at[slot], twin_landed.at[slot], head=line.twin
        ).wait_recv()
        to_twin(slot, mine).wait_send()
    pair.wait_send()


def gather_stream(partial, residual, ranks):
    halves, rows, width = partial.shape
    count = ranks // 2
    dma = pltpu.SemaphoreType.DMA
    joined = width % 128 == 0
    shape = (halves * rows, ranks * width) if joined else (halves, ranks, rows, width)
    stream = pl.pallas_call(
        functools.partial(stream_kernel, ranks),
        out_shape=jax.ShapeDtypeStruct(shape, partial.dtype),
        in_specs=[pl.BlockSpec(memory_space=pltpu.VMEM)] * 2,
        out_specs=pl.BlockSpec(memory_space=pltpu.VMEM),
        scratch_shapes=[
            pltpu.VMEM((rows, width), partial.dtype),
            pltpu.VMEM((rows, width), partial.dtype),
            dma((count,)), dma((count,)), dma((count,)), dma((ranks,)), dma((2,)), dma((ranks,)), dma((ranks,)),
        ],
        compiler_params=pltpu.CompilerParams(
            collective_id=1, has_side_effects=True, vmem_limit_bytes=40 * 2**20
        ),
        name="gather_stream",
    )(partial, residual)
    if joined:
        return stream
    return stream.transpose(0, 2, 1, 3).reshape(halves * rows, ranks * width)


def sums_kernel(
    ranks, partial, out, twin_part, acc, from_across, from_down, from_up, work, give, got,
    twin_sent, twin_landed, across_sent, across_landed, up_sent, up_landed, down_sent, down_landed,
    sum_sent, sum_landed, last_sem,
):
    line = Line(ranks)
    count = line.count
    line.greet(True)
    wide = jnp.float32

    def to_twin(block):
        return send(
            partial.at[line.twin, block], twin_part.at[block],
            twin_sent.at[block], twin_landed.at[block], head=line.twin,
        )

    def to_across(s):
        return send(
            acc.at[2 * s + 1 - line.y], from_across.at[s],
            across_sent.at[s], across_landed.at[s], blk=line.across,
        )

    def to_up(s):
        return send(
            acc.at[2 * s + line.y], from_down.at[s], up_sent.at[s], up_landed.at[s], blk=line.up
        )

    def to_down(s):
        return send(
            acc.at[2 * s + line.y], from_up.at[s], down_sent.at[s], down_landed.at[s], blk=line.down
        )

    def pair_sum(block):
        to_twin(block).wait_recv()
        acc[block] = (partial[line.head, block].astype(wide) + twin_part[block].astype(wide)).astype(
            acc.dtype
        )

    def add(block, ref):
        acc[block] = (acc[block].astype(wide) + ref.astype(wide)).astype(acc.dtype)

    order = []
    for s in range(count):
        far = count - 1 - s // 2 if s % 2 == 0 else s // 2
        order.append(far)
    for s in order:
        to_twin(2 * s + 1 - line.y).start()
    to_twin(ranks).start()
    for s in order:
        to_twin(2 * s + line.y).start()
    for s in order:
        pair_sum(2 * s + 1 - line.y)
        to_across(s).start()
    pair_sum(ranks)
    sums = LineSum(line, lambda: acc[ranks], work, sum_sent, sum_landed)
    sums.step(0)
    for s in order:
        pair_sum(2 * s + line.y)
        to_across(s).wait_recv()
        add(2 * s + line.y, from_across[s])

        @pl.when(s > line.z)
        def _():
            @pl.when(line.has_down)
            def _():
                to_up(s).wait_recv()
                add(2 * s + line.y, from_down[s])

            to_up(s).start()

        @pl.when(s < line.z)
        def _():
            @pl.when(line.has_up)
            def _():
                to_down(s).wait_recv()
                add(2 * s + line.y, from_up[s])

            to_down(s).start()

    for step in range(1, count):
        sums.step(step)
    sums.column()
    sums.across().start()

    @pl.when(line.has_down)
    def _():
        to_up(line.z).wait_recv()
        add(line.rank, from_down[line.z])

    @pl.when(line.has_up)
    def _():
        to_down(line.z).wait_recv()
        add(line.rank, from_up[line.z])

    spare = sums.total()
    mine = acc[line.rank].astype(wide)
    first = line.head == 0
    give[...] = jnp.where(first, spare, mine).astype(give.dtype)
    last = send(give, got, last_sem.at[0], last_sem.at[1], head=line.twin)
    last.start()
    out[line.head] = jnp.where(first, mine, spare).astype(out.dtype)
    last.wait_recv()
    out[line.twin] = got[...]
    last.wait_send()
    sums.drain()
    for block in range(ranks + 1):
        to_twin(block).wait_send()
    for s in range(count):
        to_across(s).wait_send()
        pl.when(s > line.z)(lambda: to_up(s).wait_send())
        pl.when(s < line.z)(lambda: to_down(s).wait_send())


def scatter_sums(partial, ranks):
    halves, blocks, rows, width = partial.shape
    count = ranks // 2
    dma = pltpu.SemaphoreType.DMA

    def held(*lead):
        return pltpu.VMEM((*lead, rows, width), partial.dtype)

    return pl.pallas_call(
        functools.partial(sums_kernel, ranks),
        out_shape=jax.ShapeDtypeStruct((halves, rows, width), partial.dtype),
        in_specs=[pl.BlockSpec(memory_space=pltpu.VMEM)],
        out_specs=pl.BlockSpec(memory_space=pltpu.VMEM),
        scratch_shapes=[
            held(blocks), held(blocks), held(count), held(count), held(count), held(6), held(), held(),
            dma((blocks,)), dma((blocks,)),
            dma((count,)), dma((count,)), dma((count,)), dma((count,)), dma((count,)), dma((count,)),
            dma((3,)), dma((3,)), dma((2,)),
        ],
        compiler_params=pltpu.CompilerParams(
            collective_id=2, has_side_effects=True, vmem_limit_bytes=48 * 2**20
        ),
        name="scatter_sums",
    )(partial)


def on_device(
    queries,
    latent_cache,
    new_latent,
    span_len,
    dec_count,
    span_start,
    cache_len,
    value_weight,
    out_weight,
    residual,
    norm_gain,
    gate_weight,
    up_weight,
    down_weight,
):
    rank_index = lax.axis_index("blk")
    rows_dev = residual.shape[0]
    heads_here = value_weight.shape[0]
    lives = span_len + dec_count
    query_rows = queries.reshape(rows_dev, heads_here, queries.shape[1] // heads_here)
    latent_out = local_attention(
        query_rows,
        latent_cache,
        new_latent,
        pick_rank(span_len, rank_index),
        pick_rank(dec_count, rank_index),
        span_start[0],
        cache_len[0],
        value_weight.shape[1],
    )
    head_values = jnp.einsum(
        "rhl,hlv->rhv", latent_out, value_weight, preferred_element_type=jnp.float32
    )
    head_values = head_values.astype(jnp.bfloat16).reshape(
        rows_dev, heads_here * value_weight.shape[2]
    )
    first = rows_dev // 2
    half = first // 2
    is_full = pick_rank(lives, rank_index) > first
    width = out_weight.shape[1]
    ranks = lax.axis_size("blk")
    moved = lax.all_to_all(
        residual.reshape(rows_dev, ranks, width).transpose(1, 0, 2),
        "blk",
        split_axis=0,
        concat_axis=0,
        tiled=True,
    )
    full_ranks = (lives > first)[:, None, None]
    spare_residual = jnp.sum(jnp.where(full_ranks, moved[:, first:], 0).astype(jnp.float32), axis=0)
    residual_rows = jnp.concatenate(
        [moved[:, :first], spare_residual.astype(residual.dtype)[None]]
    )
    residual_rows = residual_rows.reshape(ranks + 1, 2, half, width).transpose(1, 0, 2, 3)
    residual_rows = residual_rows.reshape(2, (ranks + 1) * half, width)
    rest = jnp.where(is_full, head_values[first:], 0).astype(jnp.bfloat16)
    packed = gather_rows(
        head_values[:first].reshape(2, half, -1), rest.reshape(2, half, -1), ranks
    )
    packed = packed.reshape(2 * (ranks + 1) * half, -1)
    partial_out = jnp.dot(packed, out_weight, preferred_element_type=jnp.float32)
    partial_out = partial_out.astype(jnp.bfloat16).reshape(2, (ranks + 1) * half, width)
    stream = gather_stream(partial_out, residual_rows, ranks)
    wide = stream.astype(jnp.float32)
    scale_rows = lax.rsqrt(jnp.mean(wide * wide, axis=1, keepdims=True) + norm_eps)
    normed = (wide * scale_rows * norm_gain[None, :]).astype(jnp.bfloat16)
    gate_values = jnp.dot(normed, gate_weight, preferred_element_type=jnp.float32)
    up_values = jnp.dot(normed, up_weight, preferred_element_type=jnp.float32)
    hidden = (jax.nn.silu(gate_values) * up_values).astype(jnp.bfloat16)
    partial = jnp.dot(hidden, down_weight, preferred_element_type=jnp.float32).astype(jnp.bfloat16)
    projected = scatter_sums(partial.reshape(2, ranks + 1, half, -1), ranks)
    projected = projected.reshape(first, -1).astype(jnp.float32)
    head_index = lax.axis_index("head")
    block = jnp.where(head_index == 0, rank_index, ranks)
    stream_half = lax.dynamic_slice_in_dim(stream.reshape(2, ranks + 1, half, -1), block, 1, 1)
    stream_half = stream_half.reshape(first, -1).astype(jnp.float32)
    own_rows = head_index * first + jnp.arange(first, dtype=jnp.int32)
    alive = own_rows < pick_rank(lives, rank_index)
    return jnp.where(alive[:, None], stream_half + projected, 0.0).astype(jnp.bfloat16)


def solution(mesh):
    placed = (
        P(("groups", "blk"), "head"),
        P(("groups", "blk"), None, None),
        P(None, ("groups", "blk")),
        P("groups"),
        P("groups"),
        P(("groups", "blk")),
        P(("groups", "blk"), None),
        P("head", None, None),
        P("head", "blk"),
        P(("groups", "blk"), None),
        P(),
        P(None, ("blk", "head")),
        P(None, ("blk", "head")),
        P(("blk", "head"), None),
    )
    return jax.shard_map(
        on_device,
        mesh=mesh,
        in_specs=placed,
        out_specs=P(("groups", "blk", "head"), None),
        check_vma=False,
    )
```

```python
import jax
import jax.numpy as jnp
from jax import lax
from jax.experimental import pallas as pl
from jax.experimental.pallas import tpu as pltpu
from jax.sharding import PartitionSpec as P
import functools

score_scale = 192.0 ** (-0.5)
norm_eps = 1e-06
masked_score = -1e30


def rounded(values):
    return lax.optimization_barrier(values.astype(jnp.bfloat16)).astype(jnp.float32)


def pick_rank(values, rank_index):
    matches = jnp.arange(values.shape[0], dtype=jnp.int32) == rank_index
    return jnp.sum(jnp.where(matches, values, 0))


def local_attention(
    query_rows, cache_slots, fresh_keys, span_rows, decode_rows, start_pos, lengths, key_width
):
    row_count = query_rows.shape[0]
    slot_count = cache_slots.shape[0]
    positions = jnp.arange(cache_slots.shape[2], dtype=jnp.int32)
    local_rows = jnp.arange(row_count, dtype=jnp.int32)
    cached_scores = (
        jnp.einsum("rhl,lt->rht", query_rows, cache_slots[0], preferred_element_type=jnp.float32)
        * score_scale
    )
    fresh_scores = (
        jnp.einsum("rhl,lj->rhj", query_rows, fresh_keys, preferred_element_type=jnp.float32)
        * score_scale
    )
    cached_seen = (positions < start_pos)[None, None, :]
    fresh_seen = (local_rows[None, :] <= local_rows[:, None])[:, None, :]
    cached_scores = jnp.where(cached_seen, cached_scores, masked_score)
    fresh_scores = jnp.where(fresh_seen, fresh_scores, masked_score)
    peak_score = jnp.maximum(jnp.max(cached_scores, axis=2), jnp.max(fresh_scores, axis=2))[
        :, :, None
    ]
    cached_exp = jnp.where(cached_seen, jnp.exp(cached_scores - peak_score), 0.0)
    fresh_exp = jnp.where(fresh_seen, jnp.exp(fresh_scores - peak_score), 0.0)
    totals = jnp.sum(cached_exp, axis=2, keepdims=True) + jnp.sum(fresh_exp, axis=2, keepdims=True)
    span_out = jnp.einsum(
        "rht,lt->rhl",
        (cached_exp / totals).astype(jnp.bfloat16),
        cache_slots[0, :key_width],
        preferred_element_type=jnp.float32,
    )
    span_out = span_out + jnp.einsum(
        "rhj,lj->rhl",
        (fresh_exp / totals).astype(jnp.bfloat16),
        fresh_keys[:key_width],
        preferred_element_type=jnp.float32,
    )
    decode_slots = jnp.arange(slot_count - 1, dtype=jnp.int32)
    decode_index = jnp.clip(span_rows + decode_slots, 0, row_count - 1)
    decode_query = jnp.take(query_rows, decode_index, axis=0)
    decode_keys = cache_slots[1:]
    own_keys = jnp.take(fresh_keys, decode_index, axis=1)
    slot_scores = (
        jnp.einsum("shl,slt->sht", decode_query, decode_keys, preferred_element_type=jnp.float32)
        * score_scale
    )
    slot_seen = (positions[None, :] < lengths[:, None])[:, None, :]
    slot_scores = jnp.where(slot_seen, slot_scores, masked_score)
    own_scores = (
        jnp.einsum("shl,ls->sh", decode_query, own_keys, preferred_element_type=jnp.float32)
        * score_scale
    )
    slot_peak = jnp.maximum(jnp.max(slot_scores, axis=2), own_scores)
    slot_exp = jnp.where(slot_seen, jnp.exp(slot_scores - slot_peak[:, :, None]), 0.0)
    own_exp = jnp.exp(own_scores - slot_peak)
    slot_totals = jnp.sum(slot_exp, axis=2) + own_exp
    decode_out = jnp.einsum(
        "sht,slt->shl",
        (slot_exp / slot_totals[:, :, None]).astype(jnp.bfloat16),
        decode_keys[:, :key_width],
        preferred_element_type=jnp.float32,
    )
    decode_out = (
        decode_out
        + rounded(own_exp / slot_totals)[:, :, None]
        * own_keys[:key_width].T.astype(jnp.float32)[:, None, :]
    )
    placing = (
        (local_rows[:, None] == span_rows + decode_slots[None, :])
        & (decode_slots[None, :] < decode_rows)
    ).astype(jnp.float32)
    latent_out = jnp.where((local_rows < span_rows)[:, None, None], span_out, 0.0)
    latent_out = latent_out + jnp.einsum("is,shl->ihl", placing, decode_out)
    return latent_out.astype(jnp.bfloat16)


def send(src, dst, sent, landed, **device):
    return pltpu.make_async_remote_copy(
        src_ref=src,
        dst_ref=dst,
        send_sem=sent,
        recv_sem=landed,
        device_id=device,
        device_id_type=pl.DeviceIdType.MESH,
    )


class Line:
    def __init__(self, ranks):
        self.rank = lax.axis_index("blk")
        self.head = lax.axis_index("head")
        self.count = ranks // 2
        self.z = lax.div(self.rank, 2)
        self.y = lax.rem(self.rank, 2)
        self.has_up = self.z < self.count - 1
        self.has_down = self.z > 0
        self.up = self.rank + 2
        self.down = self.rank - 2
        self.across = self.rank + 1 - 2 * self.y
        self.twin = 1 - self.head

    def greet(self, with_twin):
        barrier = pltpu.get_barrier_semaphore()

        def signal(**device):
            pl.semaphore_signal(
                barrier, inc=1, device_id=device, device_id_type=pl.DeviceIdType.MESH
            )

        signal(blk=self.across)
        if with_twin:
            signal(head=self.twin)
        pl.when(self.has_up)(lambda: signal(blk=self.up))
        pl.when(self.has_down)(lambda: signal(blk=self.down))
        ends = (self.z == 0).astype(jnp.int32) + (self.z == self.count - 1).astype(jnp.int32)
        pl.semaphore_wait(barrier, (4 if with_twin else 3) - ends)


def gather_ranks(line, own, place, up_sem, down_sem, across_sem, landed, arrived, between):
    def to_up(s, src):
        slot = 2 * s + line.y
        return send(src, place(slot), up_sem.at[s], landed.at[slot], blk=line.up)

    def to_down(s, src):
        slot = 2 * s + line.y
        return send(src, place(slot), down_sem.at[s], landed.at[slot], blk=line.down)

    def to_across(s, src):
        slot = 2 * s + line.y
        return send(src, place(slot), across_sem.at[s], landed.at[slot], blk=line.across)

    pl.when(line.has_up)(lambda: to_up(line.z, own).start())
    pl.when(line.has_down)(lambda: to_down(line.z, own).start())
    to_across(line.z, own).start()
    for step in range(1, line.count):
        low, high = line.z - step, line.z + step
        between(step)

        @pl.when(low >= 0)
        def _():
            held = place(2 * low + line.y)
            to_up(low, held).wait_recv()
            pl.when(line.has_up)(lambda: to_up(low, held).start())
            to_across(low, held).start()
            arrived(2 * low + line.y)

        @pl.when(high < line.count)
        def _():
            held = place(2 * high + line.y)
            to_down(high, held).wait_recv()
            pl.when(line.has_down)(lambda: to_down(high, held).start())
            to_across(high, held).start()
            arrived(2 * high + line.y)

    for s in range(line.count):
        slot = 2 * s + 1 - line.y
        send(place(slot), place(slot), across_sem.at[s], landed.at[slot], blk=line.across).wait_recv()
        arrived(slot)
    for s in range(line.count):
        held = place(2 * s + line.y)
        to_across(s, held).wait_send()
        pl.when(line.has_up & (s <= line.z))(lambda: to_up(s, held).wait_send())
        pl.when(line.has_down & (s >= line.z))(lambda: to_down(s, held).wait_send())


class LineSum:
    def __init__(self, line, own, work, sent, landed):
        self.line, self.own, self.work, self.sent, self.landed = line, own, work, sent, landed

    def copy(self, src, kind, **device):
        return send(
            self.work.at[src], self.work.at[kind], self.sent.at[kind], self.landed.at[kind], **device
        )

    def step(self, index):
        line = self.line

        @pl.when(line.z == index)
        def _():
            self.work[3] = self.own()
            if index > 0:
                self.copy(3, 0, blk=line.up).wait_recv()
                self.work[3] = self.work[3] + self.work[0]
            pl.when(line.has_up)(lambda: self.copy(3, 0, blk=line.up).start())

        @pl.when(line.z == line.count - 1 - index)
        def _():
            self.work[4] = self.own()
            if index > 0:
                self.copy(4, 1, blk=line.down).wait_recv()
                self.work[4] = self.work[4] + self.work[1]
            pl.when(line.has_down)(lambda: self.copy(4, 1, blk=line.down).start())

    def column(self):
        self.work[5] = (
            self.work[3].astype(jnp.float32)
            + self.work[4].astype(jnp.float32)
            - self.own().astype(jnp.float32)
        ).astype(self.work.dtype)

    def across(self):
        return self.copy(5, 2, blk=self.line.across)

    def total(self):
        self.across().wait_recv()
        return self.work[5].astype(jnp.float32) + self.work[2].astype(jnp.float32)

    def drain(self):
        line = self.line
        self.across().wait_send()
        pl.when(line.has_up)(lambda: self.copy(3, 0, blk=line.up).wait_send())
        pl.when(line.has_down)(lambda: self.copy(4, 1, blk=line.down).wait_send())


def rows_kernel(ranks, own, rest, out, work, up_sem, down_sem, across_sem, landed, sum_sent, sum_landed):
    line = Line(ranks)
    line.greet(False)
    sums = LineSum(line, lambda: rest[...], work, sum_sent, sum_landed)
    sums.step(0)
    out[:, line.rank] = own[...]

    def between(step):
        sums.step(step)
        if step == line.count - 1:
            sums.column()
            sums.across().start()

    gather_ranks(
        line, own, lambda slot: out.at[:, slot], up_sem, down_sem, across_sem, landed,
        lambda slot: None, between,
    )
    out[:, ranks] = sums.total().astype(out.dtype)
    sums.drain()


def gather_rows(own, rest, ranks):
    halves, rows, width = own.shape
    count = ranks // 2
    dma = pltpu.SemaphoreType.DMA
    return pl.pallas_call(
        functools.partial(rows_kernel, ranks),
        out_shape=jax.ShapeDtypeStruct((halves, ranks + 1, rows, width), own.dtype),
        in_specs=[pl.BlockSpec(memory_space=pltpu.VMEM)] * 2,
        out_specs=pl.BlockSpec(memory_space=pltpu.VMEM),
        scratch_shapes=[
            pltpu.VMEM((6, halves, rows, width), own.dtype),
            dma((count,)), dma((count,)), dma((count,)), dma((ranks,)), dma((3,)), dma((3,)),
        ],
        compiler_params=pltpu.CompilerParams(
            collective_id=0, has_side_effects=True, vmem_limit_bytes=40 * 2**20
        ),
        name="gather_rows",
    )(own, rest)


def stream_kernel(
    ranks, partial, residual, out, other, mine, up_sem, down_sem, across_sem, landed, pair_sem, twin_sent, twin_landed
):
    line = Line(ranks)
    line.greet(True)
    rows, width = mine.shape
    pair = send(partial.at[line.twin], other, pair_sem.at[0], pair_sem.at[1], head=line.twin)
    pair.start()
    pair.wait_recv()
    mine[...] = (
        residual[line.head].astype(jnp.float32)
        + partial[line.head].astype(jnp.float32)
        + other[...].astype(jnp.float32)
    ).astype(mine.dtype)

    def spot(head, slot):
        if len(out.shape) == 4:
            return head, slot
        return (
            pl.ds(pl.multiple_of(head * rows, rows), rows),
            pl.ds(pl.multiple_of(slot * width, width), width),
        )

    def place(head, slot):
        return out.at[spot(head, slot)]

    def to_twin(slot, src):
        return send(
            src, place(line.head, slot), twin_sent.at[slot], twin_landed.at[slot], head=line.twin
        )

    def arrived(slot):
        to_twin(slot, place(line.head, slot)).start()

    to_twin(line.rank, mine).start()
    out[spot(line.head, line.rank)] = mine[...]
    gather_ranks(
        line, mine, lambda slot: place(line.head, slot), up_sem, down_sem, across_sem, landed,
        arrived, lambda step: None,
    )
    for slot in range(ranks):
        send(
            mine, place(line.twin, slot), twin_sent.at[slot], twin_landed.at[slot], head=line.twin
        ).wait_recv()
        to_twin(slot, mine).wait_send()
    pair.wait_send()


def gather_stream(partial, residual, ranks):
    halves, rows, width = partial.shape
    count = ranks // 2
    dma = pltpu.SemaphoreType.DMA
    joined = width % 128 == 0
    shape = (halves * rows, ranks * width) if joined else (halves, ranks, rows, width)
    stream = pl.pallas_call(
        functools.partial(stream_kernel, ranks),
        out_shape=jax.ShapeDtypeStruct(shape, partial.dtype),
        in_specs=[pl.BlockSpec(memory_space=pltpu.VMEM)] * 2,
        out_specs=pl.BlockSpec(memory_space=pltpu.VMEM),
        scratch_shapes=[
            pltpu.VMEM((rows, width), partial.dtype),
            pltpu.VMEM((rows, width), partial.dtype),
            dma((count,)), dma((count,)), dma((count,)), dma((ranks,)), dma((2,)), dma((ranks,)), dma((ranks,)),
        ],
        compiler_params=pltpu.CompilerParams(
            collective_id=1, has_side_effects=True, vmem_limit_bytes=40 * 2**20
        ),
        name="gather_stream",
    )(partial, residual)
    if joined:
        return stream
    return stream.transpose(0, 2, 1, 3).reshape(halves * rows, ranks * width)


def sums_kernel(
    ranks, partial, out, twin_part, acc, from_across, from_down, from_up, work, give, got,
    twin_sent, twin_landed, across_sent, across_landed, up_sent, up_landed, down_sent, down_landed,
    sum_sent, sum_landed, last_sem,
):
    line = Line(ranks)
    count = line.count
    line.greet(True)
    wide = jnp.float32

    def to_twin(block):
        return send(
            partial.at[line.twin, block], twin_part.at[block],
            twin_sent.at[block], twin_landed.at[block], head=line.twin,
        )

    def to_across(s):
        return send(
            acc.at[2 * s + 1 - line.y], from_across.at[s],
            across_sent.at[s], across_landed.at[s], blk=line.across,
        )

    def to_up(s):
        return send(
            acc.at[2 * s + line.y], from_down.at[s], up_sent.at[s], up_landed.at[s], blk=line.up
        )

    def to_down(s):
        return send(
            acc.at[2 * s + line.y], from_up.at[s], down_sent.at[s], down_landed.at[s], blk=line.down
        )

    def pair_sum(block):
        to_twin(block).wait_recv()
        acc[block] = (partial[line.head, block].astype(wide) + twin_part[block].astype(wide)).astype(
            acc.dtype
        )

    def add(block, ref):
        acc[block] = (acc[block].astype(wide) + ref.astype(wide)).astype(acc.dtype)

    order = []
    for s in range(count):
        far = count - 1 - s // 2 if s % 2 == 0 else s // 2
        order.append(far)
    to_twin(ranks).start()
    for s in order:
        to_twin(2 * s + 1 - line.y).start()
    for s in order:
        to_twin(2 * s + line.y).start()
    pair_sum(ranks)
    sums = LineSum(line, lambda: acc[ranks], work, sum_sent, sum_landed)
    sums.step(0)
    for s in order:
        pair_sum(2 * s + 1 - line.y)
        to_across(s).start()
    for index, s in enumerate(order):
        pair_sum(2 * s + line.y)
        if index > 0:
            sums.step(index)
        if index == count - 1:
            sums.column()
            sums.across().start()
        to_across(s).wait_recv()
        add(2 * s + line.y, from_across[s])

        @pl.when(s > line.z)
        def _():
            @pl.when(line.has_down)
            def _():
                to_up(s).wait_recv()
                add(2 * s + line.y, from_down[s])

            to_up(s).start()

        @pl.when(s < line.z)
        def _():
            @pl.when(line.has_up)
            def _():
                to_down(s).wait_recv()
                add(2 * s + line.y, from_up[s])

            to_down(s).start()

    @pl.when(line.has_down)
    def _():
        to_up(line.z).wait_recv()
        add(line.rank, from_down[line.z])

    @pl.when(line.has_up)
    def _():
        to_down(line.z).wait_recv()
        add(line.rank, from_up[line.z])

    spare = sums.total()
    mine = acc[line.rank].astype(wide)
    first = line.head == 0
    give[...] = jnp.where(first, spare, mine).astype(give.dtype)
    last = send(give, got, last_sem.at[0], last_sem.at[1], head=line.twin)
    last.start()
    out[line.head] = jnp.where(first, mine, spare).astype(out.dtype)
    last.wait_recv()
    out[line.twin] = got[...]
    last.wait_send()
    sums.drain()
    for block in range(ranks + 1):
        to_twin(block).wait_send()
    for s in range(count):
        to_across(s).wait_send()
        pl.when(s > line.z)(lambda: to_up(s).wait_send())
        pl.when(s < line.z)(lambda: to_down(s).wait_send())


def scatter_sums(partial, ranks):
    halves, blocks, rows, width = partial.shape
    count = ranks // 2
    dma = pltpu.SemaphoreType.DMA

    def held(*lead):
        return pltpu.VMEM((*lead, rows, width), partial.dtype)

    return pl.pallas_call(
        functools.partial(sums_kernel, ranks),
        out_shape=jax.ShapeDtypeStruct((halves, rows, width), partial.dtype),
        in_specs=[pl.BlockSpec(memory_space=pltpu.VMEM)],
        out_specs=pl.BlockSpec(memory_space=pltpu.VMEM),
        scratch_shapes=[
            held(blocks), held(blocks), held(count), held(count), held(count), held(6), held(), held(),
            dma((blocks,)), dma((blocks,)),
            dma((count,)), dma((count,)), dma((count,)), dma((count,)), dma((count,)), dma((count,)),
            dma((3,)), dma((3,)), dma((2,)),
        ],
        compiler_params=pltpu.CompilerParams(
            collective_id=2, has_side_effects=True, vmem_limit_bytes=48 * 2**20
        ),
        name="scatter_sums",
    )(partial)


def mlp_kernel(steps, features, x, gain, gate, up, down, out, gate_sum, up_sum, squares, hidden):
    step = pl.program_id(0)

    @pl.when(step == 0)
    def _():
        gate_sum[...] = jnp.zeros_like(gate_sum)
        up_sum[...] = jnp.zeros_like(up_sum)
        squares[...] = jnp.zeros_like(squares)

    @pl.when(step < steps)
    def _():
        wide = x[...].astype(jnp.float32)
        squares[...] += jnp.sum(wide * wide, axis=1, keepdims=True)
        scaled = (wide * gain[...]).astype(x.dtype)
        gate_sum[...] += jnp.dot(scaled, gate[...], preferred_element_type=jnp.float32)
        up_sum[...] += jnp.dot(scaled, up[...], preferred_element_type=jnp.float32)

    @pl.when(step == steps - 1)
    def _():
        scale = lax.rsqrt(squares[...] / features + norm_eps)
        gate_values = gate_sum[...] * scale
        silu = gate_values / (1.0 + jnp.exp(-gate_values))
        hidden[...] = (silu * (up_sum[...] * scale)).astype(hidden.dtype)

    @pl.when(step >= steps)
    def _():
        out[...] = jnp.dot(hidden[...], down[...], preferred_element_type=jnp.float32).astype(out.dtype)


def mlp_partial(stream, gain, gate, up, down):
    rows, features = stream.shape
    units = gate.shape[1]
    tile = next(size for size in (1024, 512, 256, 128, features) if features % size == 0)
    steps = features // tile

    def early(step):
        return jnp.minimum(step, steps - 1)

    def late(step):
        return jnp.maximum(step - steps, 0)

    return pl.pallas_call(
        functools.partial(mlp_kernel, steps, features),
        grid=(2 * steps,),
        out_shape=jax.ShapeDtypeStruct((rows, features), stream.dtype),
        in_specs=[
            pl.BlockSpec((rows, tile), lambda i: (0, early(i))),
            pl.BlockSpec((1, tile), lambda i: (0, early(i))),
            pl.BlockSpec((tile, units), lambda i: (early(i), 0)),
            pl.BlockSpec((tile, units), lambda i: (early(i), 0)),
            pl.BlockSpec((units, tile), lambda i: (0, late(i))),
        ],
        out_specs=pl.BlockSpec((rows, tile), lambda i: (0, late(i))),
        scratch_shapes=[
            pltpu.VMEM((rows, units), jnp.float32),
            pltpu.VMEM((rows, units), jnp.float32),
            pltpu.VMEM((rows, 1), jnp.float32),
            pltpu.VMEM((rows, units), stream.dtype),
        ],
        compiler_params=pltpu.CompilerParams(
            dimension_semantics=("arbitrary",), vmem_limit_bytes=40 * 2**20
        ),
        name="mlp_partial",
    )(stream, gain[None, :], gate, up, down)


def on_device(
    queries,
    latent_cache,
    new_latent,
    span_len,
    dec_count,
    span_start,
    cache_len,
    value_weight,
    out_weight,
    residual,
    norm_gain,
    gate_weight,
    up_weight,
    down_weight,
):
    rank_index = lax.axis_index("blk")
    rows_dev = residual.shape[0]
    heads_here = value_weight.shape[0]
    lives = span_len + dec_count
    query_rows = queries.reshape(rows_dev, heads_here, queries.shape[1] // heads_here)
    latent_out = local_attention(
        query_rows,
        latent_cache,
        new_latent,
        pick_rank(span_len, rank_index),
        pick_rank(dec_count, rank_index),
        span_start[0],
        cache_len[0],
        value_weight.shape[1],
    )
    head_values = jnp.einsum(
        "rhl,hlv->rhv", latent_out, value_weight, preferred_element_type=jnp.float32
    )
    head_values = head_values.astype(jnp.bfloat16).reshape(
        rows_dev, heads_here * value_weight.shape[2]
    )
    first = rows_dev // 2
    half = first // 2
    is_full = pick_rank(lives, rank_index) > first
    width = out_weight.shape[1]
    ranks = lax.axis_size("blk")
    moved = lax.all_to_all(
        residual.reshape(rows_dev, ranks, width).transpose(1, 0, 2),
        "blk",
        split_axis=0,
        concat_axis=0,
        tiled=True,
    )
    full_ranks = (lives > first)[:, None, None]
    spare_residual = jnp.sum(jnp.where(full_ranks, moved[:, first:], 0).astype(jnp.float32), axis=0)
    residual_rows = jnp.concatenate(
        [moved[:, :first], spare_residual.astype(residual.dtype)[None]]
    )
    residual_rows = residual_rows.reshape(ranks + 1, 2, half, width).transpose(1, 0, 2, 3)
    residual_rows = residual_rows.reshape(2, (ranks + 1) * half, width)
    rest = jnp.where(is_full, head_values[first:], 0).astype(jnp.bfloat16)
    packed = gather_rows(
        head_values[:first].reshape(2, half, -1), rest.reshape(2, half, -1), ranks
    )
    packed = packed.reshape(2 * (ranks + 1) * half, -1)
    partial_out = jnp.dot(packed, out_weight, preferred_element_type=jnp.float32)
    partial_out = partial_out.astype(jnp.bfloat16).reshape(2, (ranks + 1) * half, width)
    stream = gather_stream(partial_out, residual_rows, ranks)
    partial = mlp_partial(stream, norm_gain, gate_weight, up_weight, down_weight)
    projected = scatter_sums(partial.reshape(2, ranks + 1, half, -1), ranks)
    projected = projected.reshape(first, -1).astype(jnp.float32)
    head_index = lax.axis_index("head")
    block = jnp.where(head_index == 0, rank_index, ranks)
    stream_half = lax.dynamic_slice_in_dim(stream.reshape(2, ranks + 1, half, -1), block, 1, 1)
    stream_half = stream_half.reshape(first, -1).astype(jnp.float32)
    own_rows = head_index * first + jnp.arange(first, dtype=jnp.int32)
    alive = own_rows < pick_rank(lives, rank_index)
    return jnp.where(alive[:, None], stream_half + projected, 0.0).astype(jnp.bfloat16)


def solution(mesh):
    placed = (
        P(("groups", "blk"), "head"),
        P(("groups", "blk"), None, None),
        P(None, ("groups", "blk")),
        P("groups"),
        P("groups"),
        P(("groups", "blk")),
        P(("groups", "blk"), None),
        P("head", None, None),
        P("head", "blk"),
        P(("groups", "blk"), None),
        P(),
        P(None, ("blk", "head")),
        P(None, ("blk", "head")),
        P(("blk", "head"), None),
    )
    return jax.shard_map(
        on_device,
        mesh=mesh,
        in_specs=placed,
        out_specs=P(("groups", "blk", "head"), None),
        check_vma=False,
    )
```

```python
import jax
import jax.numpy as jnp
from jax import lax
from jax.experimental import pallas as pl
from jax.experimental.pallas import tpu as pltpu
from jax.sharding import PartitionSpec as P
import functools

score_scale = 192.0 ** (-0.5)
norm_eps = 1e-06
masked_score = -1e30


def rounded(values):
    return lax.optimization_barrier(values.astype(jnp.bfloat16)).astype(jnp.float32)


def pick_rank(values, rank_index):
    matches = jnp.arange(values.shape[0], dtype=jnp.int32) == rank_index
    return jnp.sum(jnp.where(matches, values, 0))


def local_attention(
    query_rows, cache_slots, fresh_keys, span_rows, decode_rows, start_pos, lengths, key_width
):
    row_count = query_rows.shape[0]
    slot_count = cache_slots.shape[0]
    positions = jnp.arange(cache_slots.shape[2], dtype=jnp.int32)
    local_rows = jnp.arange(row_count, dtype=jnp.int32)
    cached_scores = (
        jnp.einsum("rhl,lt->rht", query_rows, cache_slots[0], preferred_element_type=jnp.float32)
        * score_scale
    )
    fresh_scores = (
        jnp.einsum("rhl,lj->rhj", query_rows, fresh_keys, preferred_element_type=jnp.float32)
        * score_scale
    )
    cached_seen = (positions < start_pos)[None, None, :]
    fresh_seen = (local_rows[None, :] <= local_rows[:, None])[:, None, :]
    cached_scores = jnp.where(cached_seen, cached_scores, masked_score)
    fresh_scores = jnp.where(fresh_seen, fresh_scores, masked_score)
    peak_score = jnp.maximum(jnp.max(cached_scores, axis=2), jnp.max(fresh_scores, axis=2))[
        :, :, None
    ]
    cached_exp = jnp.where(cached_seen, jnp.exp(cached_scores - peak_score), 0.0)
    fresh_exp = jnp.where(fresh_seen, jnp.exp(fresh_scores - peak_score), 0.0)
    totals = jnp.sum(cached_exp, axis=2, keepdims=True) + jnp.sum(fresh_exp, axis=2, keepdims=True)
    span_out = jnp.einsum(
        "rht,lt->rhl",
        (cached_exp / totals).astype(jnp.bfloat16),
        cache_slots[0, :key_width],
        preferred_element_type=jnp.float32,
    )
    span_out = span_out + jnp.einsum(
        "rhj,lj->rhl",
        (fresh_exp / totals).astype(jnp.bfloat16),
        fresh_keys[:key_width],
        preferred_element_type=jnp.float32,
    )
    decode_slots = jnp.arange(slot_count - 1, dtype=jnp.int32)
    decode_index = jnp.clip(span_rows + decode_slots, 0, row_count - 1)
    decode_query = jnp.take(query_rows, decode_index, axis=0)
    decode_keys = cache_slots[1:]
    own_keys = jnp.take(fresh_keys, decode_index, axis=1)
    slot_scores = (
        jnp.einsum("shl,slt->sht", decode_query, decode_keys, preferred_element_type=jnp.float32)
        * score_scale
    )
    slot_seen = (positions[None, :] < lengths[:, None])[:, None, :]
    slot_scores = jnp.where(slot_seen, slot_scores, masked_score)
    own_scores = (
        jnp.einsum("shl,ls->sh", decode_query, own_keys, preferred_element_type=jnp.float32)
        * score_scale
    )
    slot_peak = jnp.maximum(jnp.max(slot_scores, axis=2), own_scores)
    slot_exp = jnp.where(slot_seen, jnp.exp(slot_scores - slot_peak[:, :, None]), 0.0)
    own_exp = jnp.exp(own_scores - slot_peak)
    slot_totals = jnp.sum(slot_exp, axis=2) + own_exp
    decode_out = jnp.einsum(
        "sht,slt->shl",
        (slot_exp / slot_totals[:, :, None]).astype(jnp.bfloat16),
        decode_keys[:, :key_width],
        preferred_element_type=jnp.float32,
    )
    decode_out = (
        decode_out
        + rounded(own_exp / slot_totals)[:, :, None]
        * own_keys[:key_width].T.astype(jnp.float32)[:, None, :]
    )
    placing = (
        (local_rows[:, None] == span_rows + decode_slots[None, :])
        & (decode_slots[None, :] < decode_rows)
    ).astype(jnp.float32)
    latent_out = jnp.where((local_rows < span_rows)[:, None, None], span_out, 0.0)
    latent_out = latent_out + jnp.einsum("is,shl->ihl", placing, decode_out)
    return latent_out.astype(jnp.bfloat16)


def send(src, dst, sent, landed, **device):
    return pltpu.make_async_remote_copy(
        src_ref=src,
        dst_ref=dst,
        send_sem=sent,
        recv_sem=landed,
        device_id=device,
        device_id_type=pl.DeviceIdType.MESH,
    )


class Line:
    def __init__(self, ranks):
        self.rank = lax.axis_index("blk")
        self.head = lax.axis_index("head")
        self.count = ranks // 2
        self.z = lax.div(self.rank, 2)
        self.y = lax.rem(self.rank, 2)
        self.has_up = self.z < self.count - 1
        self.has_down = self.z > 0
        self.up = self.rank + 2
        self.down = self.rank - 2
        self.across = self.rank + 1 - 2 * self.y
        self.twin = 1 - self.head

    def greet(self, with_twin):
        barrier = pltpu.get_barrier_semaphore()

        def signal(**device):
            pl.semaphore_signal(
                barrier, inc=1, device_id=device, device_id_type=pl.DeviceIdType.MESH
            )

        signal(blk=self.across)
        if with_twin:
            signal(head=self.twin)
        pl.when(self.has_up)(lambda: signal(blk=self.up))
        pl.when(self.has_down)(lambda: signal(blk=self.down))
        ends = (self.z == 0).astype(jnp.int32) + (self.z == self.count - 1).astype(jnp.int32)
        pl.semaphore_wait(barrier, (4 if with_twin else 3) - ends)


def gather_ranks(line, own, place, up_sem, down_sem, across_sem, landed, arrived, between):
    def to_up(s, src):
        slot = 2 * s + line.y
        return send(src, place(slot), up_sem.at[s], landed.at[slot], blk=line.up)

    def to_down(s, src):
        slot = 2 * s + line.y
        return send(src, place(slot), down_sem.at[s], landed.at[slot], blk=line.down)

    def to_across(s, src):
        slot = 2 * s + line.y
        return send(src, place(slot), across_sem.at[s], landed.at[slot], blk=line.across)

    pl.when(line.has_up)(lambda: to_up(line.z, own).start())
    pl.when(line.has_down)(lambda: to_down(line.z, own).start())
    to_across(line.z, own).start()
    for step in range(1, line.count):
        low, high = line.z - step, line.z + step
        between(step)

        @pl.when(low >= 0)
        def _():
            held = place(2 * low + line.y)
            to_up(low, held).wait_recv()
            pl.when(line.has_up)(lambda: to_up(low, held).start())
            to_across(low, held).start()
            arrived(2 * low + line.y)

        @pl.when(high < line.count)
        def _():
            held = place(2 * high + line.y)
            to_down(high, held).wait_recv()
            pl.when(line.has_down)(lambda: to_down(high, held).start())
            to_across(high, held).start()
            arrived(2 * high + line.y)

    for s in range(line.count):
        slot = 2 * s + 1 - line.y
        send(place(slot), place(slot), across_sem.at[s], landed.at[slot], blk=line.across).wait_recv()
        arrived(slot)
    for s in range(line.count):
        held = place(2 * s + line.y)
        to_across(s, held).wait_send()
        pl.when(line.has_up & (s <= line.z))(lambda: to_up(s, held).wait_send())
        pl.when(line.has_down & (s >= line.z))(lambda: to_down(s, held).wait_send())


class LineSum:
    def __init__(self, line, own, work, sent, landed):
        self.line, self.own, self.work, self.sent, self.landed = line, own, work, sent, landed

    def copy(self, src, kind, **device):
        return send(
            self.work.at[src], self.work.at[kind], self.sent.at[kind], self.landed.at[kind], **device
        )

    def step(self, index):
        line = self.line

        @pl.when(line.z == index)
        def _():
            self.work[3] = self.own()
            if index > 0:
                self.copy(3, 0, blk=line.up).wait_recv()
                self.work[3] = self.work[3] + self.work[0]
            pl.when(line.has_up)(lambda: self.copy(3, 0, blk=line.up).start())

        @pl.when(line.z == line.count - 1 - index)
        def _():
            self.work[4] = self.own()
            if index > 0:
                self.copy(4, 1, blk=line.down).wait_recv()
                self.work[4] = self.work[4] + self.work[1]
            pl.when(line.has_down)(lambda: self.copy(4, 1, blk=line.down).start())

    def column(self):
        self.work[5] = (
            self.work[3].astype(jnp.float32)
            + self.work[4].astype(jnp.float32)
            - self.own().astype(jnp.float32)
        ).astype(self.work.dtype)

    def across(self):
        return self.copy(5, 2, blk=self.line.across)

    def total(self):
        self.across().wait_recv()
        return self.work[5].astype(jnp.float32) + self.work[2].astype(jnp.float32)

    def drain(self):
        line = self.line
        self.across().wait_send()
        pl.when(line.has_up)(lambda: self.copy(3, 0, blk=line.up).wait_send())
        pl.when(line.has_down)(lambda: self.copy(4, 1, blk=line.down).wait_send())


def rows_kernel(ranks, own, rest, out, work, up_sem, down_sem, across_sem, landed, sum_sent, sum_landed):
    line = Line(ranks)
    line.greet(False)
    sums = LineSum(line, lambda: rest[...], work, sum_sent, sum_landed)
    sums.step(0)
    out[:, line.rank] = own[...]

    def between(step):
        sums.step(step)
        if step == line.count - 1:
            sums.column()
            sums.across().start()

    gather_ranks(
        line, own, lambda slot: out.at[:, slot], up_sem, down_sem, across_sem, landed,
        lambda slot: None, between,
    )
    out[:, ranks] = sums.total().astype(out.dtype)
    sums.drain()


def gather_rows(own, rest, ranks):
    halves, rows, width = own.shape
    count = ranks // 2
    dma = pltpu.SemaphoreType.DMA
    return pl.pallas_call(
        functools.partial(rows_kernel, ranks),
        out_shape=jax.ShapeDtypeStruct((halves, ranks + 1, rows, width), own.dtype),
        in_specs=[pl.BlockSpec(memory_space=pltpu.VMEM)] * 2,
        out_specs=pl.BlockSpec(memory_space=pltpu.VMEM),
        scratch_shapes=[
            pltpu.VMEM((6, halves, rows, width), own.dtype),
            dma((count,)), dma((count,)), dma((count,)), dma((ranks,)), dma((3,)), dma((3,)),
        ],
        compiler_params=pltpu.CompilerParams(
            collective_id=0, has_side_effects=True, vmem_limit_bytes=40 * 2**20
        ),
        name="gather_rows",
    )(own, rest)


def stream_kernel(
    ranks, partial, residual, out, other, mine, up_sem, down_sem, across_sem, landed, pair_sem, twin_sent, twin_landed
):
    line = Line(ranks)
    line.greet(True)
    rows, width = mine.shape
    pair = send(partial.at[line.twin], other, pair_sem.at[0], pair_sem.at[1], head=line.twin)
    pair.start()
    pair.wait_recv()
    mine[...] = (
        residual[line.head].astype(jnp.float32)
        + partial[line.head].astype(jnp.float32)
        + other[...].astype(jnp.float32)
    ).astype(mine.dtype)

    def spot(head, slot):
        if len(out.shape) == 4:
            return head, slot
        return (
            pl.ds(pl.multiple_of(head * rows, rows), rows),
            pl.ds(pl.multiple_of(slot * width, width), width),
        )

    def place(head, slot):
        return out.at[spot(head, slot)]

    def to_twin(slot, src):
        return send(
            src, place(line.head, slot), twin_sent.at[slot], twin_landed.at[slot], head=line.twin
        )

    def arrived(slot):
        to_twin(slot, place(line.head, slot)).start()

    to_twin(line.rank, mine).start()
    out[spot(line.head, line.rank)] = mine[...]
    gather_ranks(
        line, mine, lambda slot: place(line.head, slot), up_sem, down_sem, across_sem, landed,
        arrived, lambda step: None,
    )
    for slot in range(ranks):
        send(
            mine, place(line.twin, slot), twin_sent.at[slot], twin_landed.at[slot], head=line.twin
        ).wait_recv()
        to_twin(slot, mine).wait_send()
    pair.wait_send()


def gather_stream(partial, residual, ranks):
    halves, rows, width = partial.shape
    count = ranks // 2
    dma = pltpu.SemaphoreType.DMA
    joined = width % 128 == 0
    shape = (halves * rows, ranks * width) if joined else (halves, ranks, rows, width)
    stream = pl.pallas_call(
        functools.partial(stream_kernel, ranks),
        out_shape=jax.ShapeDtypeStruct(shape, partial.dtype),
        in_specs=[pl.BlockSpec(memory_space=pltpu.VMEM)] * 2,
        out_specs=pl.BlockSpec(memory_space=pltpu.VMEM),
        scratch_shapes=[
            pltpu.VMEM((rows, width), partial.dtype),
            pltpu.VMEM((rows, width), partial.dtype),
            dma((count,)), dma((count,)), dma((count,)), dma((ranks,)), dma((2,)), dma((ranks,)), dma((ranks,)),
        ],
        compiler_params=pltpu.CompilerParams(
            collective_id=1, has_side_effects=True, vmem_limit_bytes=40 * 2**20
        ),
        name="gather_stream",
    )(partial, residual)
    if joined:
        return stream
    return stream.transpose(0, 2, 1, 3).reshape(halves * rows, ranks * width)


def sums_kernel(
    ranks, partial, out, twin_part, acc, from_across, from_down, from_up, work, give, got,
    twin_sent, twin_landed, across_sent, across_landed, up_sent, up_landed, down_sent, down_landed,
    sum_sent, sum_landed, last_sem,
):
    line = Line(ranks)
    count = line.count
    line.greet(True)
    wide = jnp.float32

    def to_twin(block):
        return send(
            partial.at[line.twin, block], twin_part.at[block],
            twin_sent.at[block], twin_landed.at[block], head=line.twin,
        )

    def to_across(s):
        return send(
            acc.at[2 * s + 1 - line.y], from_across.at[s],
            across_sent.at[s], across_landed.at[s], blk=line.across,
        )

    def to_up(s):
        return send(
            acc.at[2 * s + line.y], from_down.at[s], up_sent.at[s], up_landed.at[s], blk=line.up
        )

    def to_down(s):
        return send(
            acc.at[2 * s + line.y], from_up.at[s], down_sent.at[s], down_landed.at[s], blk=line.down
        )

    def pair_sum(block):
        to_twin(block).wait_recv()
        acc[block] = (partial[line.head, block].astype(wide) + twin_part[block].astype(wide)).astype(
            acc.dtype
        )

    def add(block, ref):
        acc[block] = (acc[block].astype(wide) + ref.astype(wide)).astype(acc.dtype)

    order = []
    for s in range(count):
        far = count - 1 - s // 2 if s % 2 == 0 else s // 2
        order.append(far)
    to_twin(ranks).start()
    for s in order:
        to_twin(2 * s + 1 - line.y).start()
    for s in order:
        to_twin(2 * s + line.y).start()
    pair_sum(ranks)
    sums = LineSum(line, lambda: acc[ranks], work, sum_sent, sum_landed)
    sums.step(0)
    for s in order:
        pair_sum(2 * s + 1 - line.y)
        to_across(s).start()
    for index, s in enumerate(order):
        pair_sum(2 * s + line.y)
        if index > 0:
            sums.step(index)
        if index == count - 1:
            sums.column()
            sums.across().start()
        to_across(s).wait_recv()
        add(2 * s + line.y, from_across[s])

        @pl.when(s > line.z)
        def _():
            @pl.when(line.has_down)
            def _():
                to_up(s).wait_recv()
                add(2 * s + line.y, from_down[s])

            to_up(s).start()

        @pl.when(s < line.z)
        def _():
            @pl.when(line.has_up)
            def _():
                to_down(s).wait_recv()
                add(2 * s + line.y, from_up[s])

            to_down(s).start()

    @pl.when(line.has_down)
    def _():
        to_up(line.z).wait_recv()
        add(line.rank, from_down[line.z])

    @pl.when(line.has_up)
    def _():
        to_down(line.z).wait_recv()
        add(line.rank, from_up[line.z])

    spare = sums.total()
    mine = acc[line.rank].astype(wide)
    first = line.head == 0
    give[...] = jnp.where(first, spare, mine).astype(give.dtype)
    last = send(give, got, last_sem.at[0], last_sem.at[1], head=line.twin)
    last.start()
    out[line.head] = jnp.where(first, mine, spare).astype(out.dtype)
    last.wait_recv()
    out[line.twin] = got[...]
    last.wait_send()
    sums.drain()
    for block in range(ranks + 1):
        to_twin(block).wait_send()
    for s in range(count):
        to_across(s).wait_send()
        pl.when(s > line.z)(lambda: to_up(s).wait_send())
        pl.when(s < line.z)(lambda: to_down(s).wait_send())


def scatter_sums(partial, ranks):
    halves, blocks, rows, width = partial.shape
    count = ranks // 2
    dma = pltpu.SemaphoreType.DMA

    def held(*lead):
        return pltpu.VMEM((*lead, rows, width), partial.dtype)

    return pl.pallas_call(
        functools.partial(sums_kernel, ranks),
        out_shape=jax.ShapeDtypeStruct((halves, rows, width), partial.dtype),
        in_specs=[pl.BlockSpec(memory_space=pltpu.VMEM)],
        out_specs=pl.BlockSpec(memory_space=pltpu.VMEM),
        scratch_shapes=[
            held(blocks), held(blocks), held(count), held(count), held(count), held(6), held(), held(),
            dma((blocks,)), dma((blocks,)),
            dma((count,)), dma((count,)), dma((count,)), dma((count,)), dma((count,)), dma((count,)),
            dma((3,)), dma((3,)), dma((2,)),
        ],
        compiler_params=pltpu.CompilerParams(
            collective_id=2, has_side_effects=True, vmem_limit_bytes=48 * 2**20
        ),
        name="scatter_sums",
    )(partial)


def mlp_kernel(steps, features, x, gain, gate, up, down, out, gate_sum, up_sum, squares, hidden):
    step = pl.program_id(0)

    @pl.when(step == 0)
    def _():
        gate_sum[...] = jnp.zeros_like(gate_sum)
        up_sum[...] = jnp.zeros_like(up_sum)
        squares[...] = jnp.zeros_like(squares)

    @pl.when(step < steps)
    def _():
        wide = x[...].astype(jnp.float32)
        squares[...] += jnp.sum(wide * wide, axis=1, keepdims=True)
        scaled = (wide * gain[...]).astype(x.dtype)
        last = (((1,), (1,)), ((), ()))
        gate_sum[...] += lax.dot_general(
            scaled, gate[...], last, preferred_element_type=jnp.float32
        )
        up_sum[...] += lax.dot_general(scaled, up[...], last, preferred_element_type=jnp.float32)

    @pl.when(step == steps - 1)
    def _():
        scale = lax.rsqrt(squares[...] / features + norm_eps)
        gate_values = gate_sum[...] * scale
        silu = gate_values / (1.0 + jnp.exp(-gate_values))
        hidden[...] = (silu * (up_sum[...] * scale)).astype(hidden.dtype)

    @pl.when(step >= steps)
    def _():
        out[...] = jnp.dot(hidden[...], down[...], preferred_element_type=jnp.float32).astype(out.dtype)


def mlp_partial(stream, gain, gate, up, down):
    rows, features = stream.shape
    units = gate.shape[1]
    tile = next(size for size in (1024, 512, 256, 128, features) if features % size == 0)
    steps = features // tile

    def early(step):
        return jnp.minimum(step, steps - 1)

    def late(step):
        return jnp.maximum(step - steps, 0)

    return pl.pallas_call(
        functools.partial(mlp_kernel, steps, features),
        grid=(2 * steps,),
        out_shape=jax.ShapeDtypeStruct((rows, features), stream.dtype),
        in_specs=[
            pl.BlockSpec((rows, tile), lambda i: (0, early(i))),
            pl.BlockSpec((1, tile), lambda i: (0, early(i))),
            pl.BlockSpec((units, tile), lambda i: (0, early(i))),
            pl.BlockSpec((units, tile), lambda i: (0, early(i))),
            pl.BlockSpec((units, tile), lambda i: (0, late(i))),
        ],
        out_specs=pl.BlockSpec((rows, tile), lambda i: (0, late(i))),
        scratch_shapes=[
            pltpu.VMEM((rows, units), jnp.float32),
            pltpu.VMEM((rows, units), jnp.float32),
            pltpu.VMEM((rows, 1), jnp.float32),
            pltpu.VMEM((rows, units), stream.dtype),
        ],
        compiler_params=pltpu.CompilerParams(
            dimension_semantics=("arbitrary",), vmem_limit_bytes=40 * 2**20
        ),
        name="mlp_partial",
    )(stream, gain[None, :], gate.T, up.T, down)


def on_device(
    queries,
    latent_cache,
    new_latent,
    span_len,
    dec_count,
    span_start,
    cache_len,
    value_weight,
    out_weight,
    residual,
    norm_gain,
    gate_weight,
    up_weight,
    down_weight,
):
    rank_index = lax.axis_index("blk")
    rows_dev = residual.shape[0]
    heads_here = value_weight.shape[0]
    lives = span_len + dec_count
    query_rows = queries.reshape(rows_dev, heads_here, queries.shape[1] // heads_here)
    latent_out = local_attention(
        query_rows,
        latent_cache,
        new_latent,
        pick_rank(span_len, rank_index),
        pick_rank(dec_count, rank_index),
        span_start[0],
        cache_len[0],
        value_weight.shape[1],
    )
    head_values = jnp.einsum(
        "rhl,hlv->rhv", latent_out, value_weight, preferred_element_type=jnp.float32
    )
    head_values = head_values.astype(jnp.bfloat16).reshape(
        rows_dev, heads_here * value_weight.shape[2]
    )
    first = rows_dev // 2
    half = first // 2
    is_full = pick_rank(lives, rank_index) > first
    width = out_weight.shape[1]
    ranks = lax.axis_size("blk")
    moved = lax.all_to_all(
        residual.reshape(rows_dev, ranks, width).transpose(1, 0, 2),
        "blk",
        split_axis=0,
        concat_axis=0,
        tiled=True,
    )
    full_ranks = (lives > first)[:, None, None]
    spare_residual = jnp.sum(jnp.where(full_ranks, moved[:, first:], 0).astype(jnp.float32), axis=0)
    residual_rows = jnp.concatenate(
        [moved[:, :first], spare_residual.astype(residual.dtype)[None]]
    )
    residual_rows = residual_rows.reshape(ranks + 1, 2, half, width).transpose(1, 0, 2, 3)
    residual_rows = residual_rows.reshape(2, (ranks + 1) * half, width)
    rest = jnp.where(is_full, head_values[first:], 0).astype(jnp.bfloat16)
    packed = gather_rows(
        head_values[:first].reshape(2, half, -1), rest.reshape(2, half, -1), ranks
    )
    packed = packed.reshape(2 * (ranks + 1) * half, -1)
    partial_out = jnp.dot(packed, out_weight, preferred_element_type=jnp.float32)
    partial_out = partial_out.astype(jnp.bfloat16).reshape(2, (ranks + 1) * half, width)
    stream = gather_stream(partial_out, residual_rows, ranks)
    partial = mlp_partial(stream, norm_gain, gate_weight, up_weight, down_weight)
    projected = scatter_sums(partial.reshape(2, ranks + 1, half, -1), ranks)
    projected = projected.reshape(first, -1).astype(jnp.float32)
    head_index = lax.axis_index("head")
    block = jnp.where(head_index == 0, rank_index, ranks)
    stream_half = lax.dynamic_slice_in_dim(stream.reshape(2, ranks + 1, half, -1), block, 1, 1)
    stream_half = stream_half.reshape(first, -1).astype(jnp.float32)
    own_rows = head_index * first + jnp.arange(first, dtype=jnp.int32)
    alive = own_rows < pick_rank(lives, rank_index)
    return jnp.where(alive[:, None], stream_half + projected, 0.0).astype(jnp.bfloat16)


def solution(mesh):
    placed = (
        P(("groups", "blk"), "head"),
        P(("groups", "blk"), None, None),
        P(None, ("groups", "blk")),
        P("groups"),
        P("groups"),
        P(("groups", "blk")),
        P(("groups", "blk"), None),
        P("head", None, None),
        P("head", "blk"),
        P(("groups", "blk"), None),
        P(),
        P(None, ("blk", "head")),
        P(None, ("blk", "head")),
        P(("blk", "head"), None),
    )
    return jax.shard_map(
        on_device,
        mesh=mesh,
        in_specs=placed,
        out_specs=P(("groups", "blk", "head"), None),
        check_vma=False,
    )
```

```python
import jax
import jax.numpy as jnp
from jax import lax
from jax.experimental import pallas as pl
from jax.experimental.pallas import tpu as pltpu
from jax.sharding import PartitionSpec as P
import functools

score_scale = 192.0 ** (-0.5)
norm_eps = 1e-06
masked_score = -1e30


def rounded(values):
    return lax.optimization_barrier(values.astype(jnp.bfloat16)).astype(jnp.float32)


def pick_rank(values, rank_index):
    matches = jnp.arange(values.shape[0], dtype=jnp.int32) == rank_index
    return jnp.sum(jnp.where(matches, values, 0))


def local_attention(
    query_rows, cache_slots, fresh_keys, span_rows, decode_rows, start_pos, lengths, key_width
):
    row_count = query_rows.shape[0]
    slot_count = cache_slots.shape[0]
    positions = jnp.arange(cache_slots.shape[2], dtype=jnp.int32)
    local_rows = jnp.arange(row_count, dtype=jnp.int32)
    cached_scores = (
        jnp.einsum("rhl,lt->rht", query_rows, cache_slots[0], preferred_element_type=jnp.float32)
        * score_scale
    )
    fresh_scores = (
        jnp.einsum("rhl,lj->rhj", query_rows, fresh_keys, preferred_element_type=jnp.float32)
        * score_scale
    )
    cached_seen = (positions < start_pos)[None, None, :]
    fresh_seen = (local_rows[None, :] <= local_rows[:, None])[:, None, :]
    cached_scores = jnp.where(cached_seen, cached_scores, masked_score)
    fresh_scores = jnp.where(fresh_seen, fresh_scores, masked_score)
    peak_score = jnp.maximum(jnp.max(cached_scores, axis=2), jnp.max(fresh_scores, axis=2))[
        :, :, None
    ]
    cached_exp = jnp.where(cached_seen, jnp.exp(cached_scores - peak_score), 0.0)
    fresh_exp = jnp.where(fresh_seen, jnp.exp(fresh_scores - peak_score), 0.0)
    totals = jnp.sum(cached_exp, axis=2, keepdims=True) + jnp.sum(fresh_exp, axis=2, keepdims=True)
    span_out = jnp.einsum(
        "rht,lt->rhl",
        (cached_exp / totals).astype(jnp.bfloat16),
        cache_slots[0, :key_width],
        preferred_element_type=jnp.float32,
    )
    span_out = span_out + jnp.einsum(
        "rhj,lj->rhl",
        (fresh_exp / totals).astype(jnp.bfloat16),
        fresh_keys[:key_width],
        preferred_element_type=jnp.float32,
    )
    decode_slots = jnp.arange(slot_count - 1, dtype=jnp.int32)
    decode_index = jnp.clip(span_rows + decode_slots, 0, row_count - 1)
    decode_query = jnp.take(query_rows, decode_index, axis=0)
    decode_keys = cache_slots[1:]
    own_keys = jnp.take(fresh_keys, decode_index, axis=1)
    slot_scores = (
        jnp.einsum("shl,slt->sht", decode_query, decode_keys, preferred_element_type=jnp.float32)
        * score_scale
    )
    slot_seen = (positions[None, :] < lengths[:, None])[:, None, :]
    slot_scores = jnp.where(slot_seen, slot_scores, masked_score)
    own_scores = (
        jnp.einsum("shl,ls->sh", decode_query, own_keys, preferred_element_type=jnp.float32)
        * score_scale
    )
    slot_peak = jnp.maximum(jnp.max(slot_scores, axis=2), own_scores)
    slot_exp = jnp.where(slot_seen, jnp.exp(slot_scores - slot_peak[:, :, None]), 0.0)
    own_exp = jnp.exp(own_scores - slot_peak)
    slot_totals = jnp.sum(slot_exp, axis=2) + own_exp
    decode_out = jnp.einsum(
        "sht,slt->shl",
        (slot_exp / slot_totals[:, :, None]).astype(jnp.bfloat16),
        decode_keys[:, :key_width],
        preferred_element_type=jnp.float32,
    )
    decode_out = (
        decode_out
        + rounded(own_exp / slot_totals)[:, :, None]
        * own_keys[:key_width].T.astype(jnp.float32)[:, None, :]
    )
    placing = (
        (local_rows[:, None] == span_rows + decode_slots[None, :])
        & (decode_slots[None, :] < decode_rows)
    ).astype(jnp.float32)
    latent_out = jnp.where((local_rows < span_rows)[:, None, None], span_out, 0.0)
    latent_out = latent_out + jnp.einsum("is,shl->ihl", placing, decode_out)
    return latent_out.astype(jnp.bfloat16)


def send(src, dst, sent, landed, **device):
    return pltpu.make_async_remote_copy(
        src_ref=src,
        dst_ref=dst,
        send_sem=sent,
        recv_sem=landed,
        device_id=device,
        device_id_type=pl.DeviceIdType.MESH,
    )


class Line:
    def __init__(self, ranks):
        self.rank = lax.axis_index("blk")
        self.head = lax.axis_index("head")
        self.count = ranks // 2
        self.z = lax.div(self.rank, 2)
        self.y = lax.rem(self.rank, 2)
        self.has_up = self.z < self.count - 1
        self.has_down = self.z > 0
        self.up = self.rank + 2
        self.down = self.rank - 2
        self.across = self.rank + 1 - 2 * self.y
        self.twin = 1 - self.head

    def greet(self, with_twin):
        barrier = pltpu.get_barrier_semaphore()

        def signal(**device):
            pl.semaphore_signal(
                barrier, inc=1, device_id=device, device_id_type=pl.DeviceIdType.MESH
            )

        signal(blk=self.across)
        if with_twin:
            signal(head=self.twin)
        pl.when(self.has_up)(lambda: signal(blk=self.up))
        pl.when(self.has_down)(lambda: signal(blk=self.down))
        ends = (self.z == 0).astype(jnp.int32) + (self.z == self.count - 1).astype(jnp.int32)
        pl.semaphore_wait(barrier, (4 if with_twin else 3) - ends)


def gather_ranks(line, own, place, up_sem, down_sem, across_sem, landed, arrived, between):
    def to_up(s, src):
        slot = 2 * s + line.y
        return send(src, place(slot), up_sem.at[s], landed.at[slot], blk=line.up)

    def to_down(s, src):
        slot = 2 * s + line.y
        return send(src, place(slot), down_sem.at[s], landed.at[slot], blk=line.down)

    def to_across(s, src):
        slot = 2 * s + line.y
        return send(src, place(slot), across_sem.at[s], landed.at[slot], blk=line.across)

    pl.when(line.has_up)(lambda: to_up(line.z, own).start())
    pl.when(line.has_down)(lambda: to_down(line.z, own).start())
    to_across(line.z, own).start()
    for step in range(1, line.count):
        low, high = line.z - step, line.z + step
        between(step)

        @pl.when(low >= 0)
        def _():
            held = place(2 * low + line.y)
            to_up(low, held).wait_recv()
            pl.when(line.has_up)(lambda: to_up(low, held).start())
            to_across(low, held).start()
            arrived(2 * low + line.y)

        @pl.when(high < line.count)
        def _():
            held = place(2 * high + line.y)
            to_down(high, held).wait_recv()
            pl.when(line.has_down)(lambda: to_down(high, held).start())
            to_across(high, held).start()
            arrived(2 * high + line.y)

    for s in range(line.count):
        slot = 2 * s + 1 - line.y
        send(place(slot), place(slot), across_sem.at[s], landed.at[slot], blk=line.across).wait_recv()
        arrived(slot)
    for s in range(line.count):
        held = place(2 * s + line.y)
        to_across(s, held).wait_send()
        pl.when(line.has_up & (s <= line.z))(lambda: to_up(s, held).wait_send())
        pl.when(line.has_down & (s >= line.z))(lambda: to_down(s, held).wait_send())


class LineSum:
    def __init__(self, line, own, work, sent, landed):
        self.line, self.own, self.work, self.sent, self.landed = line, own, work, sent, landed

    def copy(self, src, kind, **device):
        return send(
            self.work.at[src], self.work.at[kind], self.sent.at[kind], self.landed.at[kind], **device
        )

    def step(self, index):
        line = self.line

        @pl.when(line.z == index)
        def _():
            self.work[3] = self.own()
            if index > 0:
                self.copy(3, 0, blk=line.up).wait_recv()
                self.work[3] = self.work[3] + self.work[0]
            pl.when(line.has_up)(lambda: self.copy(3, 0, blk=line.up).start())

        @pl.when(line.z == line.count - 1 - index)
        def _():
            self.work[4] = self.own()
            if index > 0:
                self.copy(4, 1, blk=line.down).wait_recv()
                self.work[4] = self.work[4] + self.work[1]
            pl.when(line.has_down)(lambda: self.copy(4, 1, blk=line.down).start())

    def column(self):
        self.work[5] = (
            self.work[3].astype(jnp.float32)
            + self.work[4].astype(jnp.float32)
            - self.own().astype(jnp.float32)
        ).astype(self.work.dtype)

    def across(self):
        return self.copy(5, 2, blk=self.line.across)

    def total(self):
        self.across().wait_recv()
        return self.work[5].astype(jnp.float32) + self.work[2].astype(jnp.float32)

    def drain(self):
        line = self.line
        self.across().wait_send()
        pl.when(line.has_up)(lambda: self.copy(3, 0, blk=line.up).wait_send())
        pl.when(line.has_down)(lambda: self.copy(4, 1, blk=line.down).wait_send())


def rows_kernel(ranks, own, rest, out, work, up_sem, down_sem, across_sem, landed, sum_sent, sum_landed):
    line = Line(ranks)
    line.greet(False)
    sums = LineSum(line, lambda: rest[...], work, sum_sent, sum_landed)
    sums.step(0)
    out[:, line.rank] = own[...]

    def between(step):
        sums.step(step)
        if step == line.count - 1:
            sums.column()
            sums.across().start()

    gather_ranks(
        line, own, lambda slot: out.at[:, slot], up_sem, down_sem, across_sem, landed,
        lambda slot: None, between,
    )
    out[:, ranks] = sums.total().astype(out.dtype)
    sums.drain()


def gather_rows(own, rest, ranks):
    halves, rows, width = own.shape
    count = ranks // 2
    dma = pltpu.SemaphoreType.DMA
    return pl.pallas_call(
        functools.partial(rows_kernel, ranks),
        out_shape=jax.ShapeDtypeStruct((halves, ranks + 1, rows, width), own.dtype),
        in_specs=[pl.BlockSpec(memory_space=pltpu.VMEM)] * 2,
        out_specs=pl.BlockSpec(memory_space=pltpu.VMEM),
        scratch_shapes=[
            pltpu.VMEM((6, halves, rows, width), own.dtype),
            dma((count,)), dma((count,)), dma((count,)), dma((ranks,)), dma((3,)), dma((3,)),
        ],
        compiler_params=pltpu.CompilerParams(
            collective_id=0, has_side_effects=True, vmem_limit_bytes=40 * 2**20
        ),
        name="gather_rows",
    )(own, rest)


def stream_kernel(
    ranks, partial, residual, out, other, mine, up_sem, down_sem, across_sem, landed, pair_sem, twin_sent, twin_landed
):
    line = Line(ranks)
    line.greet(True)
    rows, width = mine.shape
    pair = send(partial.at[line.twin], other, pair_sem.at[0], pair_sem.at[1], head=line.twin)
    pair.start()
    pair.wait_recv()
    mine[...] = (
        residual[line.head].astype(jnp.float32)
        + partial[line.head].astype(jnp.float32)
        + other[...].astype(jnp.float32)
    ).astype(mine.dtype)

    def spot(head, slot):
        if len(out.shape) == 4:
            return head, slot
        return (
            pl.ds(pl.multiple_of(head * rows, rows), rows),
            pl.ds(pl.multiple_of(slot * width, width), width),
        )

    def place(head, slot):
        return out.at[spot(head, slot)]

    def to_twin(slot, src):
        return send(
            src, place(line.head, slot), twin_sent.at[slot], twin_landed.at[slot], head=line.twin
        )

    def arrived(slot):
        to_twin(slot, place(line.head, slot)).start()

    to_twin(line.rank, mine).start()
    out[spot(line.head, line.rank)] = mine[...]
    gather_ranks(
        line, mine, lambda slot: place(line.head, slot), up_sem, down_sem, across_sem, landed,
        arrived, lambda step: None,
    )
    for slot in range(ranks):
        send(
            mine, place(line.twin, slot), twin_sent.at[slot], twin_landed.at[slot], head=line.twin
        ).wait_recv()
        to_twin(slot, mine).wait_send()
    pair.wait_send()


def gather_stream(partial, residual, ranks):
    halves, rows, width = partial.shape
    count = ranks // 2
    dma = pltpu.SemaphoreType.DMA
    joined = width % 128 == 0
    shape = (halves * rows, ranks * width) if joined else (halves, ranks, rows, width)
    stream = pl.pallas_call(
        functools.partial(stream_kernel, ranks),
        out_shape=jax.ShapeDtypeStruct(shape, partial.dtype),
        in_specs=[pl.BlockSpec(memory_space=pltpu.VMEM)] * 2,
        out_specs=pl.BlockSpec(memory_space=pltpu.VMEM),
        scratch_shapes=[
            pltpu.VMEM((rows, width), partial.dtype),
            pltpu.VMEM((rows, width), partial.dtype),
            dma((count,)), dma((count,)), dma((count,)), dma((ranks,)), dma((2,)), dma((ranks,)), dma((ranks,)),
        ],
        compiler_params=pltpu.CompilerParams(
            collective_id=1, has_side_effects=True, vmem_limit_bytes=40 * 2**20
        ),
        name="gather_stream",
    )(partial, residual)
    if joined:
        return stream
    return stream.transpose(0, 2, 1, 3).reshape(halves * rows, ranks * width)


def sums_kernel(
    ranks, partial, out, twin_part, acc, from_across, from_down, from_up, work, give, got,
    twin_sent, twin_landed, across_sent, across_landed, up_sent, up_landed, down_sent, down_landed,
    sum_sent, sum_landed, last_sem,
):
    line = Line(ranks)
    count = line.count
    line.greet(True)
    wide = jnp.float32

    def to_twin(block):
        return send(
            partial.at[line.twin, block], twin_part.at[block],
            twin_sent.at[block], twin_landed.at[block], head=line.twin,
        )

    pieces = 2
    part = out.shape[2] // pieces

    def columns(piece):
        return pl.ds(piece * part, part)

    def to_across(s, piece):
        index = s * pieces + piece
        return send(
            acc.at[2 * s + 1 - line.y, :, columns(piece)], from_across.at[s, :, columns(piece)],
            across_sent.at[index], across_landed.at[index], blk=line.across,
        )

    def to_up(s, piece):
        index = s * pieces + piece
        return send(
            acc.at[2 * s + line.y, :, columns(piece)], from_down.at[s, :, columns(piece)],
            up_sent.at[index], up_landed.at[index], blk=line.up,
        )

    def to_down(s, piece):
        index = s * pieces + piece
        return send(
            acc.at[2 * s + line.y, :, columns(piece)], from_up.at[s, :, columns(piece)],
            down_sent.at[index], down_landed.at[index], blk=line.down,
        )

    def pair_sum(block):
        to_twin(block).wait_recv()
        acc[block] = (partial[line.head, block].astype(wide) + twin_part[block].astype(wide)).astype(
            acc.dtype
        )

    def add(block, held, s, piece):
        total = acc[block, :, columns(piece)].astype(wide) + held[s, :, columns(piece)].astype(wide)
        acc[block, :, columns(piece)] = total.astype(acc.dtype)

    order = []
    for s in range(count):
        far = count - 1 - s // 2 if s % 2 == 0 else s // 2
        order.append(far)
    to_twin(ranks).start()
    for s in order:
        to_twin(2 * s + 1 - line.y).start()
    for s in order:
        to_twin(2 * s + line.y).start()
    pair_sum(ranks)
    sums = LineSum(line, lambda: acc[ranks], work, sum_sent, sum_landed)
    sums.step(0)
    for s in order:
        pair_sum(2 * s + 1 - line.y)
        for piece in range(pieces):
            to_across(s, piece).start()
    for index, s in enumerate(order):
        pair_sum(2 * s + line.y)
        if index > 0:
            sums.step(index)
        if index == count - 1:
            sums.column()
            sums.across().start()
        for piece in range(pieces):
            to_across(s, piece).wait_recv()
            add(2 * s + line.y, from_across, s, piece)

            @pl.when(s > line.z)
            def _():
                @pl.when(line.has_down)
                def _():
                    to_up(s, piece).wait_recv()
                    add(2 * s + line.y, from_down, s, piece)

                to_up(s, piece).start()

            @pl.when(s < line.z)
            def _():
                @pl.when(line.has_up)
                def _():
                    to_down(s, piece).wait_recv()
                    add(2 * s + line.y, from_up, s, piece)

                to_down(s, piece).start()

    for piece in range(pieces):

        @pl.when(line.has_down)
        def _():
            to_up(line.z, piece).wait_recv()
            add(line.rank, from_down, line.z, piece)

        @pl.when(line.has_up)
        def _():
            to_down(line.z, piece).wait_recv()
            add(line.rank, from_up, line.z, piece)

    spare = sums.total()
    mine = acc[line.rank].astype(wide)
    first = line.head == 0
    give[...] = jnp.where(first, spare, mine).astype(give.dtype)
    last = send(give, got, last_sem.at[0], last_sem.at[1], head=line.twin)
    last.start()
    out[line.head] = jnp.where(first, mine, spare).astype(out.dtype)
    last.wait_recv()
    out[line.twin] = got[...]
    last.wait_send()
    sums.drain()
    for block in range(ranks + 1):
        to_twin(block).wait_send()
    for s in range(count):
        for piece in range(pieces):
            to_across(s, piece).wait_send()
            pl.when(s > line.z)(lambda: to_up(s, piece).wait_send())
            pl.when(s < line.z)(lambda: to_down(s, piece).wait_send())


def scatter_sums(partial, ranks):
    halves, blocks, rows, width = partial.shape
    count = ranks // 2
    dma = pltpu.SemaphoreType.DMA

    def held(*lead):
        return pltpu.VMEM((*lead, rows, width), partial.dtype)

    return pl.pallas_call(
        functools.partial(sums_kernel, ranks),
        out_shape=jax.ShapeDtypeStruct((halves, rows, width), partial.dtype),
        in_specs=[pl.BlockSpec(memory_space=pltpu.VMEM)],
        out_specs=pl.BlockSpec(memory_space=pltpu.VMEM),
        scratch_shapes=[
            held(blocks), held(blocks), held(count), held(count), held(count), held(6), held(), held(),
            dma((blocks,)), dma((blocks,)),
            *[dma((2 * count,))] * 6,
            dma((3,)), dma((3,)), dma((2,)),
        ],
        compiler_params=pltpu.CompilerParams(
            collective_id=2, has_side_effects=True, vmem_limit_bytes=48 * 2**20
        ),
        name="scatter_sums",
    )(partial)


def mlp_kernel(steps, features, x, gain, gate, up, down, out, gate_sum, up_sum, squares, hidden):
    step = pl.program_id(0)

    @pl.when(step == 0)
    def _():
        gate_sum[...] = jnp.zeros_like(gate_sum)
        up_sum[...] = jnp.zeros_like(up_sum)
        squares[...] = jnp.zeros_like(squares)

    @pl.when(step < steps)
    def _():
        wide = x[...].astype(jnp.float32)
        squares[...] += jnp.sum(wide * wide, axis=1, keepdims=True)
        scaled = (wide * gain[...]).astype(x.dtype)
        last = (((1,), (1,)), ((), ()))
        gate_sum[...] += lax.dot_general(
            scaled, gate[...], last, preferred_element_type=jnp.float32
        )
        up_sum[...] += lax.dot_general(scaled, up[...], last, preferred_element_type=jnp.float32)

    @pl.when(step == steps - 1)
    def _():
        scale = lax.rsqrt(squares[...] / features + norm_eps)
        gate_values = gate_sum[...] * scale
        silu = gate_values / (1.0 + jnp.exp(-gate_values))
        hidden[...] = (silu * (up_sum[...] * scale)).astype(hidden.dtype)

    @pl.when(step >= steps)
    def _():
        out[...] = jnp.dot(hidden[...], down[...], preferred_element_type=jnp.float32).astype(out.dtype)


def mlp_partial(stream, gain, gate, up, down):
    rows, features = stream.shape
    units = gate.shape[1]
    tile = next(size for size in (1024, 512, 256, 128, features) if features % size == 0)
    steps = features // tile

    def early(step):
        return jnp.minimum(step, steps - 1)

    def late(step):
        return jnp.maximum(step - steps, 0)

    return pl.pallas_call(
        functools.partial(mlp_kernel, steps, features),
        grid=(2 * steps,),
        out_shape=jax.ShapeDtypeStruct((rows, features), stream.dtype),
        in_specs=[
            pl.BlockSpec((rows, tile), lambda i: (0, early(i))),
            pl.BlockSpec((1, tile), lambda i: (0, early(i))),
            pl.BlockSpec((units, tile), lambda i: (0, early(i))),
            pl.BlockSpec((units, tile), lambda i: (0, early(i))),
            pl.BlockSpec((units, tile), lambda i: (0, late(i))),
        ],
        out_specs=pl.BlockSpec((rows, tile), lambda i: (0, late(i))),
        scratch_shapes=[
            pltpu.VMEM((rows, units), jnp.float32),
            pltpu.VMEM((rows, units), jnp.float32),
            pltpu.VMEM((rows, 1), jnp.float32),
            pltpu.VMEM((rows, units), stream.dtype),
        ],
        compiler_params=pltpu.CompilerParams(
            dimension_semantics=("arbitrary",), vmem_limit_bytes=40 * 2**20
        ),
        name="mlp_partial",
    )(stream, gain[None, :], gate.T, up.T, down)


def on_device(
    queries,
    latent_cache,
    new_latent,
    span_len,
    dec_count,
    span_start,
    cache_len,
    value_weight,
    out_weight,
    residual,
    norm_gain,
    gate_weight,
    up_weight,
    down_weight,
):
    rank_index = lax.axis_index("blk")
    rows_dev = residual.shape[0]
    heads_here = value_weight.shape[0]
    lives = span_len + dec_count
    query_rows = queries.reshape(rows_dev, heads_here, queries.shape[1] // heads_here)
    latent_out = local_attention(
        query_rows,
        latent_cache,
        new_latent,
        pick_rank(span_len, rank_index),
        pick_rank(dec_count, rank_index),
        span_start[0],
        cache_len[0],
        value_weight.shape[1],
    )
    head_values = jnp.einsum(
        "rhl,hlv->rhv", latent_out, value_weight, preferred_element_type=jnp.float32
    )
    head_values = head_values.astype(jnp.bfloat16).reshape(
        rows_dev, heads_here * value_weight.shape[2]
    )
    first = rows_dev // 2
    half = first // 2
    is_full = pick_rank(lives, rank_index) > first
    width = out_weight.shape[1]
    ranks = lax.axis_size("blk")
    moved = lax.all_to_all(
        residual.reshape(rows_dev, ranks, width).transpose(1, 0, 2),
        "blk",
        split_axis=0,
        concat_axis=0,
        tiled=True,
    )
    full_ranks = (lives > first)[:, None, None]
    spare_residual = jnp.sum(jnp.where(full_ranks, moved[:, first:], 0).astype(jnp.float32), axis=0)
    residual_rows = jnp.concatenate(
        [moved[:, :first], spare_residual.astype(residual.dtype)[None]]
    )
    residual_rows = residual_rows.reshape(ranks + 1, 2, half, width).transpose(1, 0, 2, 3)
    residual_rows = residual_rows.reshape(2, (ranks + 1) * half, width)
    rest = jnp.where(is_full, head_values[first:], 0).astype(jnp.bfloat16)
    packed = gather_rows(
        head_values[:first].reshape(2, half, -1), rest.reshape(2, half, -1), ranks
    )
    packed = packed.reshape(2 * (ranks + 1) * half, -1)
    partial_out = jnp.dot(packed, out_weight, preferred_element_type=jnp.float32)
    partial_out = partial_out.astype(jnp.bfloat16).reshape(2, (ranks + 1) * half, width)
    stream = gather_stream(partial_out, residual_rows, ranks)
    partial = mlp_partial(stream, norm_gain, gate_weight, up_weight, down_weight)
    projected = scatter_sums(partial.reshape(2, ranks + 1, half, -1), ranks)
    projected = projected.reshape(first, -1).astype(jnp.float32)
    head_index = lax.axis_index("head")
    block = jnp.where(head_index == 0, rank_index, ranks)
    stream_half = lax.dynamic_slice_in_dim(stream.reshape(2, ranks + 1, half, -1), block, 1, 1)
    stream_half = stream_half.reshape(first, -1).astype(jnp.float32)
    own_rows = head_index * first + jnp.arange(first, dtype=jnp.int32)
    alive = own_rows < pick_rank(lives, rank_index)
    return jnp.where(alive[:, None], stream_half + projected, 0.0).astype(jnp.bfloat16)


def solution(mesh):
    placed = (
        P(("groups", "blk"), "head"),
        P(("groups", "blk"), None, None),
        P(None, ("groups", "blk")),
        P("groups"),
        P("groups"),
        P(("groups", "blk")),
        P(("groups", "blk"), None),
        P("head", None, None),
        P("head", "blk"),
        P(("groups", "blk"), None),
        P(),
        P(None, ("blk", "head")),
        P(None, ("blk", "head")),
        P(("blk", "head"), None),
    )
    return jax.shard_map(
        on_device,
        mesh=mesh,
        in_specs=placed,
        out_specs=P(("groups", "blk", "head"), None),
        check_vma=False,
    )
```
